32 devices in a mesh: ctx: 16 (over z, y, core), head: 2 (over x).
Axes of the slice: x: 2, y: 2, z: 4, core: 2. Of those that a mesh axis runs over, the one named last changes fastest.
Arguments:
- queries: bfloat16 [12288, 1024], P(('ctx', 'head')), may hold values from -64 to 64
- keys: bfloat16 [12288, 256], P(('ctx', 'head')), may hold values from -6 to 6
- values: bfloat16 [12288, 256], P(('ctx', 'head')), may hold values from -6 to 6
- out_grad: bfloat16 [12288, 1024], P(('ctx', 'head')), may hold values from -6 to 6
- rand_blocks: int32 [96, 3], replicated, may hold values from 0 to 95, as said below
- rand_count: int32 [96], replicated, may hold values from 1 to 3
Outputs:
- query_grad: bfloat16 [12288, 1024], P('ctx', 'head')
- key_grad: bfloat16 [12288, 256], P('ctx', 'head')
- value_grad: bfloat16 [12288, 256], P('ctx', 'head')
The draws below stay inside these ranges and needn't reach their ends.
Inputs may be any that keep to these rules, and one draw needn't show every extreme that they name: Entry rand_blocks[b, r] names a block of a ctx shard (a range of 6 blocks) that is neither b's own shard nor either neighbour of it, counted modulo 16. The 18 entries of one shard's query blocks name blocks of one other shard at most 2 times, exactly 2 times for some shard.
All inputs are finite; a program needn't handle non-finite values.
Results may differ from the reference program's by a relative error of at most 0.0087.
Values may be sent and summed in bfloat16 or wider, within the bound.
A program may use at most 64 MiB of HBM per device.

```python
import math
import jax
import jax.numpy as jnp
from jax import lax

BLOCK = 128
HD = 128
GROUP = 4
G = 2
RAND = 3
QB_DEV = 6
KV_HEADS = 2
HEADS = 8
NKB = 8
NQB = 96
TOKENS = 12288
N_CTX = 16


def shared_fields(key):
    folded = jax.random.fold_in(key, 101)
    field_key, query_key = jax.random.split(folded)
    key_width = KV_HEADS * HD
    key_field = jnp.clip(jax.random.normal(field_key, (TOKENS, key_width), jnp.float32), -6.0, 6.0)
    query_field = jnp.clip(jax.random.normal(query_key, (TOKENS, GROUP * key_width), jnp.float32), -6.0, 6.0)
    return (query_field, key_field)


def draw_queries(key, part):
    return shared_fields(key)[0].astype(jnp.bfloat16)


def draw_keys(key, part):
    return shared_fields(key)[1].astype(jnp.bfloat16)


def draw_rand_blocks(key, part):
    folded = jax.random.fold_in(key, 202)
    first_key, second_key, third_key = jax.random.split(folded, 3)
    entries = QB_DEV * RAND
    owners_used = min(entries, N_CTX - 3)
    candidates = jax.vmap(lambda single: jax.random.permutation(single, N_CTX - 3))(jax.random.split(first_key, N_CTX))
    shard_index = jnp.arange(N_CTX, dtype=jnp.int32)[:, None]
    candidates = (shard_index + 2 + candidates.astype(jnp.int32)) % N_CTX
    shuffle = jax.vmap(lambda single: jax.random.permutation(single, entries))(jax.random.split(second_key, N_CTX))
    slot_index = shuffle.astype(jnp.int32) % owners_used
    owners = jnp.take_along_axis(candidates, slot_index, axis=1)
    offset = jax.random.randint(third_key, (N_CTX, entries), 0, QB_DEV, dtype=jnp.int32)
    blocks = owners * QB_DEV + offset
    return blocks.reshape(NQB, RAND).astype(jnp.int32)


def plant(values, rng, low, largest):
    dims = values.shape
    spot = [jax.random.randint(jax.random.fold_in(rng, axis), (), 0, dims[axis]) for axis in range(len(dims))]
    values = values.at[tuple(spot)].set(low)
    longest = dims.index(max(dims))
    spot[longest] = (spot[longest] + 1) % dims[longest]
    return values.at[tuple(spot)].set(largest)


def shard_levels(rng, shape, cuts, low, top_value):
    factor_of = 1.0
    for dim, shards_of in cuts:
        steps = jax.random.uniform(jax.random.fold_in(jax.random.fold_in(rng, 6), dim), (shards_of,), jnp.float32, low / len(cuts), top_value / len(cuts))
        factor_of = factor_of * jnp.repeat(jnp.exp(steps), shape[dim] // shards_of).reshape((-1,) + (1,) * (len(shape) - 1 - dim))
    return factor_of


def centred(own_key, extent, scale, most, shards=(), held_as=jnp.bfloat16):
    drawn = scale * jax.random.normal(own_key, extent, jnp.float32)
    if shards:
        drawn = drawn * shard_levels(own_key, extent, shards, -0.22, 0.18)
    return jnp.clip(drawn, -most, most).astype(held_as)


def setup_inputs(seed: int = 0) -> dict:
    key_list = jax.random.split(jax.random.key(seed), 7)
    return {
        "queries": draw_queries(jax.random.fold_in(key_list[6], 71), 0),
        "keys": draw_keys(jax.random.fold_in(key_list[6], 71), 0),
        "values": centred(key_list[2], (TOKENS, KV_HEADS * HD), 1.0, 6.0, ((0, 32),)),
        "out_grad": centred(key_list[3], (TOKENS, HEADS * HD), 1.0, 6.0, ((0, 32),)),
        "rand_blocks": draw_rand_blocks(jax.random.fold_in(key_list[6], 71), 0),
        "rand_count": plant(jax.random.randint(key_list[5], (NQB,), 1, RAND + 1), jax.random.fold_in(key_list[5], 1), 1, RAND).astype(jnp.int32),
    }


def attend_block(query_tile, grad_tile, key_tile, value_tile, key_mask):
    factor = 1.0 / math.sqrt(HD)
    scores = jnp.einsum('tgh,kh->tgk', query_tile, key_tile) * factor
    scores = jnp.where(key_mask[None, None, :], scores, -jnp.inf)
    row_max = lax.optimization_barrier(jnp.max(scores, axis=-1, keepdims=True))
    raw_weights = jnp.exp(scores - row_max)
    weights = raw_weights / lax.optimization_barrier(jnp.sum(raw_weights, axis=-1, keepdims=True))
    weights_low = weights.astype(jnp.bfloat16).astype(jnp.float32)
    output = jnp.einsum('tgk,kh->tgh', weights_low, value_tile)
    row_dot = lax.optimization_barrier(jnp.sum(grad_tile * output, axis=-1, keepdims=True))
    dprobs = jnp.einsum('tgh,kh->tgk', grad_tile, value_tile)
    dscores = (weights * (dprobs - row_dot)).astype(jnp.bfloat16).astype(jnp.float32)
    dquery = (jnp.einsum('tgk,kh->tgh', dscores, key_tile) * factor).astype(jnp.bfloat16)
    key_part = jnp.einsum('tgk,tgh->kh', dscores, query_tile) * factor
    value_part = jnp.einsum('tgk,tgh->kh', weights_low, grad_tile)
    return (dquery, key_part, value_part)

def reference(queries, keys, values, out_grad, rand_blocks, rand_count):
    nblocks = rand_blocks.shape[0]
    query_all = queries.reshape(nblocks, BLOCK, KV_HEADS, GROUP, HD)
    grad_all = out_grad.reshape(nblocks, BLOCK, KV_HEADS, GROUP, HD)
    key_all = keys.reshape(nblocks, BLOCK, KV_HEADS, HD)
    value_all = values.reshape(nblocks, BLOCK, KV_HEADS, HD)
    dq_heads = []
    dk_heads = []
    dv_heads = []
    for head_id in range(KV_HEADS):
        query_head = query_all[:, :, head_id]
        grad_head = grad_all[:, :, head_id]
        key_head = key_all[:, :, head_id]
        value_head = value_all[:, :, head_id]

        def settle(part, remote):
            lowered = lax.optimization_barrier(part.astype(jnp.bfloat16)).astype(jnp.float32)
            return jnp.where(remote[:, None, None], lowered, part)

        def step(carry, block_id):
            key_acc, value_acc = carry
            window = jnp.stack([block_id - 1, block_id, block_id + 1]).astype(jnp.int32)
            key_table = jnp.concatenate([window, jnp.arange(G, dtype=jnp.int32), rand_blocks[block_id].astype(jnp.int32)])
            key_table = jnp.clip(key_table, 0, nblocks - 1)
            key_valid = jnp.concatenate([jnp.stack([block_id >= 1, block_id >= 0, block_id + 1 < nblocks]), jnp.ones((G,), bool), jnp.arange(RAND, dtype=jnp.int32) < rand_count[block_id]])
            remote = jnp.concatenate([jnp.stack([block_id % QB_DEV == 0, block_id < 0, block_id % QB_DEV == QB_DEV - 1]), jnp.zeros((G,), bool), jnp.ones((RAND,), bool)])
            key_tile = key_head[key_table].reshape(NKB * BLOCK, HD).astype(jnp.float32)
            value_tile = value_head[key_table].reshape(NKB * BLOCK, HD).astype(jnp.float32)
            key_mask = jnp.repeat(key_valid, BLOCK)
            query_tile = query_head[block_id].astype(jnp.float32)
            grad_tile = grad_head[block_id].astype(jnp.float32)
            dquery, key_part, value_part = attend_block(query_tile, grad_tile, key_tile, value_tile, key_mask)
            key_part = settle(key_part.reshape(NKB, BLOCK, HD), remote)
            value_part = settle(value_part.reshape(NKB, BLOCK, HD), remote)
            key_acc = key_acc.at[key_table].add(key_part)
            value_acc = value_acc.at[key_table].add(value_part)
            return ((key_acc, value_acc), dquery)
        zeros_acc = jnp.zeros((nblocks, BLOCK, HD), jnp.float32)
        (key_acc, value_acc), dq_blocks = lax.scan(step, (zeros_acc, zeros_acc), jnp.arange(nblocks, dtype=jnp.int32))
        dq_heads.append(dq_blocks)
        dk_heads.append(key_acc)
        dv_heads.append(value_acc)
    query_grad = jnp.stack(dq_heads, axis=2).reshape(nblocks * BLOCK, KV_HEADS * GROUP * HD)
    key_grad = jnp.stack(dk_heads, axis=2).reshape(nblocks * BLOCK, KV_HEADS * HD).astype(jnp.bfloat16)
    value_grad = jnp.stack(dv_heads, axis=2).reshape(nblocks * BLOCK, KV_HEADS * HD).astype(jnp.bfloat16)
    return (query_grad, key_grad, value_grad)
```

```python
import math

import jax
import jax.numpy as jnp
from jax import lax
from jax.experimental import pallas as pl
from jax.experimental.pallas import tpu as pltpu
from jax.sharding import PartitionSpec as P

BLOCK = 128
HD = 128
GROUP = 4
G = 2
RAND = 3
QB_DEV = 6
NKB = 8
FACTOR = 1.0 / math.sqrt(HD)
EXP_FACTOR = FACTOR * math.log2(math.e)
CONTRACT_LAST = (((1,), (1,)), ((), ()))
CONTRACT_FIRST = (((0,), (0,)), ((), ()))
CONTRACT_MATMUL = (((1,), (0,)), ((), ()))


def dot(a, b, dims=CONTRACT_MATMUL):
    return lax.dot_general(a, b, dims, preferred_element_type=jnp.float32)


def attend_kernel(
    table, valid, query_ref, grad_ref, pool_hbm,
    dquery_ref, local_ref, far_ref, total, scores, dprobs, dscores, keys, held, sems,
):
    step = pl.program_id(0)
    per_dev = local_ref.shape[0]
    entry = [table[step, e] for e in range(NKB)]
    use = [valid[step, e] > 0 for e in range(NKB)]

    @pl.when(step == 0)
    def _():
        load = pltpu.make_async_copy(pool_hbm, held, sems.at[0])
        load.start()
        total[...] = jnp.zeros_like(total)
        load.wait()

    query = jnp.concatenate([query_ref[:, h * HD : (h + 1) * HD] for h in range(GROUP)], axis=0)
    grad = jnp.concatenate([grad_ref[:, h * HD : (h + 1) * HD] for h in range(GROUP)], axis=0)
    rows = [slice(e * BLOCK, (e + 1) * BLOCK) for e in range(NKB)]
    row_max = None
    for e in range(NKB):
        key_tile = held[entry[e], :, :HD]
        keys[rows[e], :] = key_tile
        tile = dot(key_tile, query, CONTRACT_LAST)
        if use[e] is not True:
            tile += jnp.where(use[e], 0.0, -jnp.inf).astype(jnp.float32)
        scores[rows[e], :] = tile
        tile_max = jnp.max(tile, axis=0, keepdims=True)
        row_max = tile_max if e == 0 else jnp.maximum(row_max, tile_max)
    row_sum = jnp.zeros_like(row_max)
    row_dot = jnp.zeros_like(row_max)
    for e in range(NKB):
        weight = jnp.exp2((scores[rows[e], :] - row_max) * EXP_FACTOR)
        dprob = dot(held[entry[e], :, HD:], grad, CONTRACT_LAST)
        row_sum += jnp.sum(weight, axis=0, keepdims=True)
        row_dot += jnp.sum(weight * dprob, axis=0, keepdims=True)
        scores[rows[e], :] = weight
        dprobs[rows[e], :] = dprob
    scale = 1.0 / row_sum
    row_dot = row_dot * scale
    for e in range(NKB):
        weight = scores[rows[e], :] * scale
        dscore = (weight * (dprobs[rows[e], :] - row_dot)).astype(jnp.bfloat16)
        dscores[rows[e], :] = dscore
        total[entry[e], :, :HD] += dot(dscore, query) * FACTOR
        total[entry[e], :, HD:] += dot(weight.astype(jnp.bfloat16), grad)
    dquery = dot(keys[...], dscores[...], CONTRACT_FIRST) * FACTOR
    for h in range(GROUP):
        dquery_ref[:, h * HD : (h + 1) * HD] = dquery[:, h * BLOCK : (h + 1) * BLOCK].T.astype(
            jnp.bfloat16
        )

    @pl.when(step == pl.num_programs(0) - 1)
    def _():
        local_ref[...] = total[:per_dev]
        skip = total.shape[0] - far_ref.shape[0]

        @pl.loop(0, far_ref.shape[0])
        def _(i):
            held[i] = total[skip + i].astype(jnp.bfloat16)
            pltpu.make_async_copy(held.at[i], far_ref.at[i], sems.at[1]).start()

        pltpu.make_async_copy(held.at[pl.ds(0, far_ref.shape[0])], far_ref, sems.at[1]).wait()


def attend(table, valid, queries, grads, pool):
    pool_size = pool.shape[0]
    per_dev = QB_DEV
    far_size = pool_size - per_dev
    anywhere = pl.BlockSpec(memory_space=pl.ANY)
    tile = pl.BlockSpec((BLOCK, GROUP * HD), lambda i, *_: (i, 0))
    whole = lambda size: pl.BlockSpec((size, BLOCK, 2 * HD), lambda i, *_: (0, 0, 0), pipeline_mode=pl.Buffered(1))
    return pl.pallas_call(
        attend_kernel,
        grid_spec=pltpu.PrefetchScalarGridSpec(
            num_scalar_prefetch=2,
            grid=(per_dev,),
            in_specs=[tile, tile, anywhere],
            out_specs=[tile, whole(per_dev), anywhere],
            scratch_shapes=[
                pltpu.VMEM((pool_size, BLOCK, 2 * HD), jnp.float32),
                pltpu.VMEM((NKB * BLOCK, GROUP * BLOCK), jnp.float32),
                pltpu.VMEM((NKB * BLOCK, GROUP * BLOCK), jnp.float32),
                pltpu.VMEM((NKB * BLOCK, GROUP * BLOCK), jnp.bfloat16),
                pltpu.VMEM((NKB * BLOCK, HD), jnp.bfloat16),
                pltpu.VMEM((pool_size, BLOCK, 2 * HD), jnp.bfloat16),
                pltpu.SemaphoreType.DMA((2,)),
            ],
        ),
        out_shape=[
            jax.ShapeDtypeStruct(queries.shape, jnp.bfloat16),
            jax.ShapeDtypeStruct((per_dev, BLOCK, 2 * HD), jnp.float32),
            jax.ShapeDtypeStruct((far_size, BLOCK, 2 * HD), jnp.bfloat16),
        ],
        compiler_params=pltpu.CompilerParams(vmem_limit_bytes=62 << 20),
        name="attend",
    )(table, valid, queries, grads, pool)


def exchange(array):
    return lax.all_to_all(array, "ctx", split_axis=0, concat_axis=0, tiled=True)


def body(queries, keys, values, out_grad, rand_blocks, rand_count):
    heads = lax.axis_size("head")
    shards = lax.axis_size("ctx")
    myself = lax.axis_index("ctx")
    per_dev = QB_DEV
    entries = per_dev * RAND
    owners_used = min(entries, shards - 3)
    capacity = (entries + owners_used - 1) // owners_used
    total_blocks = per_dev * shards
    far_slots = shards * capacity
    piece = G * BLOCK // shards

    tokens = keys.shape[0]
    pairs = jnp.stack([keys.reshape(tokens, heads, HD), values.reshape(tokens, heads, HD)], axis=2)
    pairs = pairs.transpose(1, 0, 2, 3).reshape(heads, tokens, 2 * HD)
    local_rows = lax.all_to_all(pairs, "head", split_axis=0, concat_axis=0, tiled=True)
    local_rows = local_rows.reshape(heads * tokens, 2 * HD)
    local_pairs = local_rows.reshape(per_dev, BLOCK, 2 * HD)
    head_queries = lax.all_to_all(queries, "head", split_axis=1, concat_axis=0, tiled=True)
    head_grads = lax.all_to_all(out_grad, "head", split_axis=1, concat_axis=0, tiled=True)

    flat_blocks = rand_blocks.reshape(shards, entries)
    owners = flat_blocks // per_dev
    offsets = flat_blocks % per_dev
    positions = jnp.arange(entries, dtype=jnp.int32)
    earlier = positions[None, :] < positions[:, None]
    same_owner = owners[:, :, None] == owners[:, None, :]
    slot_ranks = jnp.sum(same_owner & earlier[None], axis=2)
    slot_range = jnp.arange(capacity, dtype=jnp.int32)
    send_hits = (
        (owners == myself)[:, None, :] & (slot_ranks[:, None, :] == slot_range[None, :, None])
    ).astype(jnp.float32)
    offset_hot = (
        offsets[:, :, None] == jnp.arange(per_dev, dtype=jnp.int32)[None, None, :]
    ).astype(jnp.float32)
    send_table = jnp.einsum("dme,deq->dmq", send_hits, offset_hot)
    targets = jnp.arange(shards, dtype=jnp.int32)[:, None, None]
    first_slot = (slot_range == 0)[None, :, None]
    block_range = jnp.arange(per_dev, dtype=jnp.int32)[None, None, :]
    right_send = (targets == (myself + 1) % shards) & first_slot & (block_range == per_dev - 1)
    left_send = (targets == (myself - 1 + shards) % shards) & first_slot & (block_range == 0)
    send_table = send_table + right_send.astype(jnp.float32) + left_send.astype(jnp.float32)
    left_far = per_dev + (myself - 1 + shards) % shards * capacity
    right_far = per_dev + (myself + 1) % shards * capacity
    outgoing = jnp.einsum(
        "dmq,qtc->dmtc",
        send_table.astype(jnp.bfloat16),
        local_pairs,
        preferred_element_type=jnp.float32,
    ).astype(jnp.bfloat16)
    pieces = local_rows[: G * BLOCK].reshape(shards, piece, 2 * HD)
    packed = jnp.concatenate([outgoing.reshape(shards, capacity * BLOCK, 2 * HD), pieces], axis=1)
    arrived = exchange(packed)
    far_pairs = arrived[:, : capacity * BLOCK].reshape(far_slots, BLOCK, 2 * HD)
    my_piece = jnp.broadcast_to(arrived[0, capacity * BLOCK :][None], (shards, piece, 2 * HD))
    global_pairs = exchange(my_piece).reshape(G, BLOCK, 2 * HD)
    pool = jnp.concatenate([local_pairs, far_pairs, global_pairs], axis=0)

    edge_base = per_dev + far_slots
    local_index = jnp.arange(per_dev, dtype=jnp.int32)
    seq_block = myself * per_dev + local_index
    left_index = jnp.where(local_index > 0, local_index - 1, left_far)
    right_index = jnp.where(local_index < per_dev - 1, local_index + 1, right_far)
    global_index = jnp.broadcast_to(
        edge_base + jnp.arange(G, dtype=jnp.int32)[None, :], (per_dev, G)
    )
    my_owners = lax.dynamic_index_in_dim(owners, myself, 0, keepdims=False)
    my_ranks = lax.dynamic_index_in_dim(slot_ranks, myself, 0, keepdims=False)
    random_index = (per_dev + my_owners * capacity + my_ranks).reshape(per_dev, RAND)
    key_table = jnp.concatenate(
        [jnp.stack([left_index, local_index, right_index], axis=1), global_index, random_index],
        axis=1,
    ).astype(jnp.int32)
    my_counts = lax.dynamic_slice_in_dim(rand_count, myself * per_dev, per_dev)
    key_valid = jnp.concatenate(
        [
            jnp.stack([seq_block > 0, seq_block >= 0, seq_block < total_blocks - 1], axis=1),
            jnp.ones((per_dev, G), bool),
            jnp.arange(RAND, dtype=jnp.int32)[None, :] < my_counts[:, None],
        ],
        axis=1,
    ).astype(jnp.int32)

    query_grad, local_grads, far_grads = attend(key_table, key_valid, head_queries, head_grads, pool)

    packed_grads = jnp.concatenate(
        [
            far_grads[:far_slots].reshape(shards, capacity * BLOCK, 2 * HD),
            far_grads[far_slots:].reshape(shards, piece, 2 * HD),
        ],
        axis=1,
    )
    returned = exchange(packed_grads)
    returned_far = returned[:, : capacity * BLOCK].reshape(shards, capacity, BLOCK, 2 * HD)
    global_piece = jnp.sum(returned[:, capacity * BLOCK :].astype(jnp.float32), axis=0)
    global_piece = jnp.broadcast_to(global_piece[None].astype(jnp.bfloat16), (shards, piece, 2 * HD))
    global_total = exchange(global_piece).reshape(G, BLOCK, 2 * HD).astype(jnp.float32)
    local_grads = local_grads + jnp.einsum(
        "dmq,dmtc->qtc",
        send_table.astype(jnp.bfloat16),
        returned_far,
        preferred_element_type=jnp.float32,
    )
    local_grads = local_grads.at[:G].add(
        jnp.where(myself == 0, global_total, jnp.zeros_like(global_total))
    )
    key_grad = local_grads[:, :, :HD].reshape(per_dev * BLOCK, HD).astype(jnp.bfloat16)
    value_grad = local_grads[:, :, HD:].reshape(per_dev * BLOCK, HD).astype(jnp.bfloat16)
    return (query_grad, key_grad, value_grad)


MESH = pl.DeviceIdType.MESH
LINE = 4
SHARD = QB_DEV * BLOCK
ENTRIES = QB_DEV * RAND
CAP = 2
SLOT = CAP * BLOCK
PAIR = 2 * HD
COLUMN = 2 * LINE
DENSE = COLUMN * QB_DEV
SPARSE = COLUMN * CAP
POOL = DENSE + SPARSE + G
WINDOW = QB_DEV + 2
HELD = WINDOW + G + ENTRIES


def place():
    me = lax.axis_index("ctx")
    return me // 4, (me // 2) % 2, me % 2


def index_of(z, y, c):
    return z * 4 + y * 2 + c


def remote(src, dst, send_sem, recv_sem, **device):
    return pltpu.make_async_remote_copy(
        src_ref=src, dst_ref=dst, send_sem=send_sem, recv_sem=recv_sem, device_id=device, device_id_type=MESH
    )


def greet(z, y, c, head):
    barrier = pltpu.get_barrier_semaphore()

    def tell(**device):
        pl.semaphore_signal(barrier, inc=1, device_id=device, device_id_type=MESH)

    tell(ctx=index_of(z, 1 - y, c))
    tell(ctx=index_of(z, 1 - y, 1 - c))
    tell(ctx=index_of(z, y, 1 - c))
    if head is not None:
        tell(head=1 - head)

    @pl.when(z > 0)
    def _():
        tell(ctx=index_of(z - 1, y, c))

    @pl.when(z < LINE - 1)
    def _():
        tell(ctx=index_of(z + 1, y, c))

    peers = (3 if head is None else 4) + (z + 2) // 3 + (5 - z) // 3
    pl.semaphore_wait(barrier, peers)


def listed(table, user, owner, missing):
    first = jnp.int32(missing)
    second = jnp.int32(missing)
    seen = jnp.int32(0)
    for e in range(ENTRIES):
        offset = table[e % RAND, user * QB_DEV + e // RAND] - owner * QB_DEV
        hit = ((offset >= 0) & (offset < QB_DEV)).astype(jnp.int32)
        second = jnp.where(hit * seen > 0, offset, second)
        first = jnp.where(hit * (1 - seen) > 0, offset, first)
        seen = jnp.maximum(seen, hit)
    first = jnp.where(user == owner + 1, QB_DEV - 1, first)
    first = jnp.where(user == owner - 1, 0, first)
    return first, second


def gather_kernel(
    table, q_in, k_in, v_in, g_in, q_out, g_out, pool,
    col, packed, local_sem, head_send, head_recv, up_send, down_send, z_recv,
    y_send, y_recv, c_send, c_recv, keep_sem, edge_send, edge_recv,
):
    z, y, c = place()
    head = lax.axis_index("head")
    other = 1 - head
    tokens = k_in.shape[0]

    def half(u):
        return pl.ds(pl.multiple_of(u * tokens, tokens), tokens)

    jobs = []
    for src, dst, width in (
        (k_in, col.at[z, half(head), :HD], HD),
        (v_in, col.at[z, half(head), HD:], HD),
        (q_in, q_out.at[half(head), :], GROUP * HD),
        (g_in, g_out.at[half(head), :], GROUP * HD),
    ):
        i = len(jobs)
        mine = src.at[:, pl.ds(pl.multiple_of(head * width, width), width)]
        theirs = src.at[:, pl.ds(pl.multiple_of(other * width, width), width)]
        jobs.append(
            (
                pltpu.make_async_copy(mine, dst, local_sem.at[i]),
                remote(theirs, dst, head_send.at[i], head_recv.at[i], head=other),
            )
        )
    for local, _ in jobs:
        local.start()
    greet(z, y, c, head)
    for _, away in jobs[:2]:
        away.start()

    def up(zz, u):
        part = col.at[zz, half(u), :]
        slot = zz * 2 + u
        return remote(part, part, up_send.at[slot], z_recv.at[slot], ctx=index_of((z + 1) % LINE, y, c))

    def down(zz, u):
        part = col.at[zz, half(u), :]
        slot = zz * 2 + u
        return remote(part, part, down_send.at[slot], z_recv.at[slot], ctx=index_of((z + 3) % LINE, y, c))

    def dense_rows(zz, cc):
        return pl.ds(pl.multiple_of((zz * 2 + cc) * SHARD, SHARD), SHARD)

    def keep(zz):
        return pltpu.make_async_copy(col.at[zz], pool.at[dense_rows(zz, c), :], keep_sem.at[zz])

    def beside(zz):
        return remote(
            col.at[zz], pool.at[dense_rows(zz, c), :], c_send.at[zz], c_recv.at[zz], ctx=index_of(z, y, 1 - c)
        )

    def across(zz, d, sender):
        start = DENSE * BLOCK + (zz * 2 + sender) * SLOT
        return remote(
            packed.at[zz, d], pool.at[pl.ds(pl.multiple_of(start, SLOT), SLOT), :],
            y_send.at[zz * 2 + d], y_recv.at[zz * 2 + sender], ctx=index_of(z, 1 - y, d),
        )

    edge_rows = pl.ds((DENSE + SPARSE) * BLOCK, G * BLOCK)

    def edge(d):
        return remote(
            col.at[0, : G * BLOCK, :], pool.at[edge_rows, :], edge_send.at[d], edge_recv.at[0],
            ctx=index_of(z, 1 - y, d),
        )

    def complete(zz):
        wanted = []
        for d in range(2):
            wanted += listed(table, index_of(z, 1 - y, d), index_of(zz, y, c), 0)

        @pl.loop(0, BLOCK // 16)
        def _(i):
            row = pl.multiple_of(i * 16, 16)
            tiles = [col[zz, pl.ds(pl.multiple_of(q * BLOCK + row, 16), 16), :] for q in range(QB_DEV)]
            for s, want in enumerate(wanted):
                tile = tiles[0]
                for q in range(1, QB_DEV):
                    tile = jnp.where(want == q, tiles[q], tile)
                packed[zz, s // CAP, pl.ds(pl.multiple_of(s % CAP * BLOCK + row, 16), 16), :] = tile

        for d in range(2):
            across(zz, d, c).start()
        beside(zz).start()
        keep(zz).start()

        @pl.when((zz == 0) & (y == 0) & (c == 0))
        def _():
            for d in range(2):
                edge(d).start()

    for local, _ in jobs[:2]:
        local.wait()

    def pass_on(zz, u, upward, downward):
        if upward:

            @pl.when(z < LINE - 1)
            def _():
                up(zz, u).start()

        if downward:

            @pl.when(z > 0)
            def _():
                down(zz, u).start()

    pass_on(z, head, True, True)
    for _, away in jobs[:2]:
        away.wait_recv()
    pass_on(z, other, True, True)
    for _, away in jobs[2:]:
        away.start()
    complete(z)

    for j in range(1, LINE):
        for u in (head, other):

            @pl.when(z - j >= 0)
            def _():
                up(z - j, u).wait_recv()
                pass_on(z - j, u, True, False)

            @pl.when(z + j <= LINE - 1)
            def _():
                down(z + j, u).wait_recv()
                pass_on(z + j, u, False, True)

        @pl.when(z - j >= 0)
        def _():
            complete(z - j)

        @pl.when(z + j <= LINE - 1)
        def _():
            complete(z + j)

    for zz in range(LINE):
        keep(zz).wait()
        beside(zz).wait_recv()
        beside(zz).wait_send()
        for d in range(2):
            across(zz, 0, d).wait_recv()
            across(zz, d, c).wait_send()
        for u in range(2):

            @pl.when((z < LINE - 1) & (zz <= z))
            def _():
                up(zz, u).wait_send()

            @pl.when((z > 0) & (zz >= z))
            def _():
                down(zz, u).wait_send()

    @pl.when(y == 1)
    def _():
        edge(0).wait_recv()

    @pl.when((y == 0) & (c == 0))
    def _():
        for d in range(2):
            edge(d).wait_send()

    for i, (local, away) in enumerate(jobs):
        if i >= 2:
            local.wait()
            away.wait_recv()
        away.wait_send()


def gather(table, queries, keys, values, grads):
    anywhere = pl.BlockSpec(memory_space=pl.ANY)
    tokens = queries.shape[0]
    moved = jax.ShapeDtypeStruct((2 * tokens, GROUP * HD), jnp.bfloat16)
    dma = pltpu.SemaphoreType.DMA
    return pl.pallas_call(
        gather_kernel,
        in_specs=[pl.BlockSpec(memory_space=pltpu.SMEM)] + [anywhere] * 4,
        out_specs=[anywhere] * 3,
        out_shape=[moved, moved, jax.ShapeDtypeStruct((POOL * BLOCK, PAIR), jnp.bfloat16)],
        scratch_shapes=[
            pltpu.VMEM((LINE, SHARD, PAIR), jnp.bfloat16),
            pltpu.VMEM((LINE, 2, SLOT, PAIR), jnp.bfloat16),
            dma((4,)), dma((4,)), dma((4,)), dma((2 * LINE,)), dma((2 * LINE,)), dma((2 * LINE,)),
            dma((2 * LINE,)), dma((2 * LINE,)), dma((LINE,)), dma((LINE,)), dma((LINE,)), dma((2,)), dma((1,)),
        ],
        compiler_params=pltpu.CompilerParams(
            collective_id=0, has_side_effects=True, vmem_limit_bytes=30 << 20
        ),
        name="gather",
    )(table, queries, keys, values, grads)


def listed_attend_kernel(
    table, count, query_ref, grad_ref, pool, dquery_ref, local_ref, slots, edges,
    held, total, scores, dprobs, dscores, sent, load_sem, send_sem,
):
    step = pl.program_id(0)
    z, y, c = place()
    me = index_of(z, y, c)
    blocks = count.shape[0]
    first = me * QB_DEV
    block = first + step

    def spot(owner, offset, rank):
        line = (owner // 4) * 2 + owner % 2
        same = (owner // 2) % 2 == y
        return jnp.where(same, line * QB_DEV + offset, DENSE + line * CAP + rank)

    def entry_of(e):
        named = table[e % RAND, first + e // RAND]
        owner = named // QB_DEV
        rank = jnp.int32(0)
        for early in range(e):
            before = table[early % RAND, first + early // RAND] // QB_DEV
            rank += (before == owner).astype(jnp.int32)
        return owner, named - owner * QB_DEV, rank

    def load(spot_of, i):
        return pltpu.make_async_copy(pool.at[spot_of], held.at[i], load_sem.at[i])

    def send(slot, i):
        return pltpu.make_async_copy(sent.at[i], slots.at[slot], send_sem.at[i])

    @pl.when(step == 0)
    def _():
        for w in range(WINDOW):
            named = jnp.minimum(jnp.maximum(first - 1 + w, 0), blocks - 1)
            owner = named // QB_DEV
            load(spot(owner, named - owner * QB_DEV, 0), w).start()
        for g in range(G):
            load(jnp.where(y == 0, g, DENSE + SPARSE + g), WINDOW + g).start()
        for e in range(ENTRIES):
            load(spot(*entry_of(e)), WINDOW + G + e).start()
        total[...] = jnp.zeros_like(total)
        load(0, 0).wait()
        load(0, 1).wait()
        for g in range(G):
            load(0, WINDOW + g).wait()

    load(0, step + 2).wait()
    for r in range(RAND):
        load(0, WINDOW + G + step * RAND + r).wait()

    entry = [step, step + 1, step + 2, WINDOW, WINDOW + 1]
    entry += [WINDOW + G + step * RAND + r for r in range(RAND)]
    use = [block > 0, True, block < blocks - 1, True, True]
    use += [r < count[block] for r in range(RAND)]

    query = jnp.concatenate([query_ref[:, h * HD : (h + 1) * HD] for h in range(GROUP)], axis=0)
    grad = jnp.concatenate([grad_ref[:, h * HD : (h + 1) * HD] for h in range(GROUP)], axis=0)
    rows = [slice(e * BLOCK, (e + 1) * BLOCK) for e in range(NKB)]
    row_max = None
    for e in range(NKB):
        tile = dot(held[entry[e], :, :HD], query, CONTRACT_LAST)
        if use[e] is not True:
            tile += jnp.where(use[e], 0.0, -jnp.inf).astype(jnp.float32)
        scores[rows[e], :] = tile
        tile_max = jnp.max(tile, axis=0, keepdims=True)
        row_max = tile_max if e == 0 else jnp.maximum(row_max, tile_max)
    row_sum = jnp.zeros_like(row_max)
    row_dot = jnp.zeros_like(row_max)
    for e in range(NKB):
        weight = jnp.exp2((scores[rows[e], :] - row_max) * EXP_FACTOR)
        dprob = dot(held[entry[e], :, HD:], grad, CONTRACT_LAST)
        row_sum += jnp.sum(weight, axis=0, keepdims=True)
        row_dot += jnp.sum(weight * dprob, axis=0, keepdims=True)
        scores[rows[e], :] = weight
        dprobs[rows[e], :] = dprob
    scale = 1.0 / row_sum
    row_dot = row_dot * scale
    dquery = None
    for e in range(NKB):
        weight = scores[rows[e], :] * scale
        dscore = (weight * (dprobs[rows[e], :] - row_dot)).astype(jnp.bfloat16)
        dscores[rows[e], :] = dscore
        dkey = dot(dscore, query) * FACTOR
        dvalue = dot(weight.astype(jnp.bfloat16), grad)
        if e < NKB - RAND:
            total[entry[e], :, :HD] += dkey
            total[entry[e], :, HD:] += dvalue
        else:
            i = step * RAND + e - (NKB - RAND)
            sent[i, :, :HD] = dkey.astype(jnp.bfloat16)
            sent[i, :, HD:] = dvalue.astype(jnp.bfloat16)
    keys = jnp.concatenate([held[entry[e], :, :HD] for e in range(NKB)], axis=0)
    dquery = dot(keys, dscores[...], CONTRACT_FIRST) * FACTOR
    for h in range(GROUP):
        dquery_ref[:, h * HD : (h + 1) * HD] = dquery[:, h * BLOCK : (h + 1) * BLOCK].T.astype(
            jnp.bfloat16
        )

    @pl.when(step == pl.num_programs(0) - 1)
    def _():
        for e in range(ENTRIES):
            owner, _, rank = entry_of(e)
            send(owner * CAP + rank, e).start()
        sent[ENTRIES] = total[0].astype(jnp.bfloat16)
        sent[ENTRIES + 1] = total[WINDOW - 1].astype(jnp.bfloat16)

        @pl.when(me > 0)
        def _():
            send((me - 1) * CAP, ENTRIES).start()

        @pl.when(me < lax.axis_size("ctx") - 1)
        def _():
            send((me + 1) * CAP, ENTRIES + 1).start()

        local_ref[...] = total[1 : WINDOW - 1]
        edges[...] = total[WINDOW:].astype(jnp.bfloat16)
        for e in range(ENTRIES):
            send(0, e).wait()

        @pl.when(me > 0)
        def _():
            send(0, ENTRIES).wait()

        @pl.when(me < lax.axis_size("ctx") - 1)
        def _():
            send(0, ENTRIES + 1).wait()


def listed_attend(table, count, queries, grads, pool):
    anywhere = pl.BlockSpec(memory_space=pl.ANY)
    tile = pl.BlockSpec((BLOCK, GROUP * HD), lambda i, *_: (i, 0))
    whole = lambda size: pl.BlockSpec((size, BLOCK, PAIR), lambda i, *_: (0, 0, 0), pipeline_mode=pl.Buffered(1))
    shards = count.shape[0] // QB_DEV
    dma = pltpu.SemaphoreType.DMA
    return pl.pallas_call(
        listed_attend_kernel,
        grid_spec=pltpu.PrefetchScalarGridSpec(
            num_scalar_prefetch=2,
            grid=(QB_DEV,),
            in_specs=[tile, tile, anywhere],
            out_specs=[tile, whole(QB_DEV), anywhere, whole(G)],
            scratch_shapes=[
                pltpu.VMEM((HELD, BLOCK, PAIR), jnp.bfloat16),
                pltpu.VMEM((WINDOW + G, BLOCK, PAIR), jnp.float32),
                pltpu.VMEM((NKB * BLOCK, GROUP * BLOCK), jnp.float32),
                pltpu.VMEM((NKB * BLOCK, GROUP * BLOCK), jnp.float32),
                pltpu.VMEM((NKB * BLOCK, GROUP * BLOCK), jnp.bfloat16),
                pltpu.VMEM((ENTRIES + 2, BLOCK, PAIR), jnp.bfloat16),
                dma((HELD,)),
                dma((ENTRIES + 2,)),
            ],
        ),
        out_shape=[
            jax.ShapeDtypeStruct(queries.shape, jnp.bfloat16),
            jax.ShapeDtypeStruct((QB_DEV, BLOCK, PAIR), jnp.float32),
            jax.ShapeDtypeStruct((shards * CAP, BLOCK, PAIR), jnp.bfloat16),
            jax.ShapeDtypeStruct((G, BLOCK, PAIR), jnp.bfloat16),
        ],
        compiler_params=pltpu.CompilerParams(vmem_limit_bytes=40 << 20),
        name="listed_attend",
    )(table, count, queries, grads, pool)


def reduce_kernel(
    table, slots, edges, local_hbm, key_grad, value_grad,
    own, beside_in, across_in, edge_in, edge_sum, local, z_out, z_in,
    own_sem, local_sem, c_send, c_recv, y_send, y_recv, edge_sem, edge_send, edge_recv, z_send, z_recv,
):
    z, y, c = place()

    def slot_rows(zz, yy, cc):
        return pl.ds(pl.multiple_of(index_of(zz, yy, cc) * SLOT, SLOT), SLOT)

    def cols(kv):
        return pl.ds(kv * HD, HD)

    def hold(zz, kv):
        return pltpu.make_async_copy(
            slots.at[slot_rows(zz, y, c), cols(kv)], own.at[zz, kv], own_sem.at[zz * 2 + kv]
        )

    def beside(zz, kv):
        i = zz * 2 + kv
        return remote(
            slots.at[slot_rows(zz, y, 1 - c), cols(kv)], beside_in.at[zz, kv],
            c_send.at[i], c_recv.at[i], ctx=index_of(z, y, 1 - c),
        )

    def across(zz, kv, d, sender):
        i = zz * 2 + kv
        return remote(
            slots.at[slot_rows(zz, 1 - y, d), cols(kv)], across_in.at[sender, zz, kv],
            y_send.at[d, i], y_recv.at[sender, i], ctx=index_of(z, 1 - y, d),
        )

    def edge(kind):
        target = index_of(z, 0, 0)
        return remote(edges, edge_in.at[kind], edge_send.at[0], edge_recv.at[kind], ctx=target)

    def up(zz, kv):
        i = zz * 2 + kv
        return remote(
            z_out.at[zz, kv], z_in.at[0, zz, kv], z_send.at[i], z_recv.at[0, i],
            ctx=index_of((z + 1) % LINE, y, c),
        )

    def down(zz, kv):
        i = zz * 2 + kv
        return remote(
            z_out.at[zz, kv], z_in.at[1, zz, kv], z_send.at[i], z_recv.at[1, i],
            ctx=index_of((z + 3) % LINE, y, c),
        )

    def pick(options):
        return jnp.where(z == 0, options[0], jnp.where(z == 1, options[1], jnp.where(z == 2, options[2], options[3])))

    order = [pick(options) for options in ((3, 3, 0, 0), (2, 0, 3, 1), (1, 2, 1, 2))] + [z]
    units = [(zz, kv) for zz in order for kv in range(2)]

    for zz, kv in units:
        hold(zz, kv).start()
    keep_edge = pltpu.make_async_copy(edges, edge_in.at[0], edge_sem.at[0])
    keep_local = pltpu.make_async_copy(local_hbm, local, local_sem.at[0])
    keep_edge.start()
    keep_local.start()
    greet(z, y, c, None)

    holder = (y == 0) & (c == 0)

    @pl.when((y == 0) & (c == 1))
    def _():
        edge(1).start()

    for d in range(2):

        @pl.when((y == 1) & (c == d))
        def _():
            edge(2 + d).start()

    for zz, kv in units:
        for d in range(2):
            across(zz, kv, d, c).start()
        beside(zz, kv).start()
    keep_edge.wait()
    edge_sum[...] = jnp.zeros_like(edge_sum)

    def take(i):
        zz, kv = units[i]
        last = i >= len(units) - 2
        hold(zz, kv).wait()
        beside(zz, kv).wait_recv()
        for d in range(2):
            across(zz, kv, 0, d).wait_recv()
        me = index_of(zz, y, c)
        wanted = []
        for user in (index_of(z, y, c), index_of(z, y, 1 - c), index_of(z, 1 - y, 0), index_of(z, 1 - y, 1)):
            wanted += listed(table, user, me, -1)
        at_edge = holder & (zz == 0)
        if i == len(units) - 2:
            keep_local.wait()
        if kv == 0:

            @pl.when(at_edge)
            def _():
                for kind in range(1, 4):
                    remote(edges, edge_in.at[kind], edge_send.at[0], edge_recv.at[kind], ctx=index_of(z, 0, 1)).wait_recv()
                edge_sum[...] = sum(edge_in[kind].astype(jnp.float32) for kind in range(4))

        def add(sides):
            @pl.loop(0, BLOCK // 16)
            def _(t):
                row = pl.multiple_of(t * 16, 16)
                tiles = []
                for ref in (own.at[zz, kv], beside_in.at[zz, kv], across_in.at[0, zz, kv], across_in.at[1, zz, kv]):
                    for k in range(CAP):
                        tiles.append(ref[pl.ds(pl.multiple_of(k * BLOCK + row, 16), 16), :].astype(jnp.float32))
                for q in range(QB_DEV):
                    rows = pl.ds(pl.multiple_of(q * BLOCK + row, 16), 16)
                    sums = None
                    if last:
                        sums = local[rows, cols(kv)]
                    for side in sides:
                        part = z_in[side, zz, kv, rows, :].astype(jnp.float32)
                        sums = part if sums is None else sums + part
                    for want, tile in zip(wanted, tiles):
                        part = jnp.where(want == q, tile, 0.0)
                        sums = part if sums is None else sums + part
                    if q < G:
                        sums += jnp.where(at_edge, edge_sum[rows, cols(kv)], 0.0)
                    sums = sums.astype(jnp.bfloat16)
                    if last and kv == 0:
                        key_grad[rows, :] = sums
                    elif last:
                        value_grad[rows, :] = sums
                    else:
                        z_out[zz, kv, rows, :] = sums

        if last:

            @pl.when(z == 0)
            def _():
                down(zz, kv).wait_recv()
                add((1,))

            @pl.when(z == LINE - 1)
            def _():
                up(zz, kv).wait_recv()
                add((0,))

            @pl.when((z > 0) & (z < LINE - 1))
            def _():
                up(zz, kv).wait_recv()
                down(zz, kv).wait_recv()
                add((0, 1))

            return

        @pl.when((z == 0) | (z == LINE - 1))
        def _():
            add(())

        @pl.when((z > 0) & (z < LINE - 1) & (zz > z))
        def _():
            up(zz, kv).wait_recv()
            add((0,))

        @pl.when((z > 0) & (z < LINE - 1) & (zz < z))
        def _():
            down(zz, kv).wait_recv()
            add((1,))

        @pl.when(zz > z)
        def _():
            up(zz, kv).start()

        @pl.when(zz < z)
        def _():
            down(zz, kv).start()

    for i in range(len(units)):
        take(i)

    for i, (zz, kv) in enumerate(units):
        beside(zz, kv).wait_send()
        for d in range(2):
            across(zz, kv, d, c).wait_send()
        if i < len(units) - 2:
            up(zz, kv).wait_send()

    @pl.when((y == 1) | (c == 1))
    def _():
        remote(edges, edge_in.at[1], edge_send.at[0], edge_recv.at[1], ctx=index_of(z, 1 - y, c)).wait_send()


def reduce(table, slots, edges, local):
    in_vmem = pl.BlockSpec(memory_space=pltpu.VMEM)
    dma = pltpu.SemaphoreType.DMA
    bf16 = jnp.bfloat16
    result = jax.ShapeDtypeStruct((SHARD, HD), jnp.bfloat16)
    return pl.pallas_call(
        reduce_kernel,
        in_specs=[pl.BlockSpec(memory_space=pltpu.SMEM)] + [pl.BlockSpec(memory_space=pl.ANY)] * 3,
        out_specs=[in_vmem] * 2,
        out_shape=[result, result],
        scratch_shapes=[
            pltpu.VMEM((LINE, 2, SLOT, HD), bf16),
            pltpu.VMEM((LINE, 2, SLOT, HD), bf16),
            pltpu.VMEM((2, LINE, 2, SLOT, HD), bf16),
            pltpu.VMEM((4, G * BLOCK, PAIR), bf16),
            pltpu.VMEM((G * BLOCK, PAIR), jnp.float32),
            pltpu.VMEM((SHARD, PAIR), jnp.float32),
            pltpu.VMEM((LINE, 2, SHARD, HD), bf16),
            pltpu.VMEM((2, LINE, 2, SHARD, HD), bf16),
            dma((2 * LINE,)), dma((1,)), dma((2 * LINE,)), dma((2 * LINE,)), dma((2, 2 * LINE)), dma((2, 2 * LINE)),
            dma((1,)), dma((1,)), dma((4,)), dma((2 * LINE,)), dma((2, 2 * LINE)),
        ],
        compiler_params=pltpu.CompilerParams(
            collective_id=1, has_side_effects=True, vmem_limit_bytes=40 << 20
        ),
        name="reduce",
    )(table, slots, edges, local)


def body_line(queries, keys, values, out_grad, rand_blocks, rand_count):
    table = rand_blocks.T
    head_queries, head_grads, pool = gather(table, queries, keys, values, out_grad)
    query_grad, local, slots, edges = listed_attend(
        table, rand_count, head_queries, head_grads, pool.reshape(POOL, BLOCK, PAIR)
    )
    key_grad, value_grad = reduce(
        table, slots.reshape(-1, PAIR), edges.reshape(-1, PAIR), local.reshape(SHARD, PAIR)
    )
    return (query_grad, key_grad, value_grad)


def solution(mesh):
    line = mesh.shape["ctx"] == 4 * LINE and mesh.shape["head"] == 2
    placed = P(("ctx", "head"), None)
    return jax.shard_map(
        body_line if line else body,
        mesh=mesh,
        in_specs=(placed, placed, placed, placed, P(), P()),
        out_specs=(P("ctx", "head"), P("ctx", "head"), P("ctx", "head")),
        check_vma=False,
    )
```

```python
import math

import jax
import jax.numpy as jnp
from jax import lax
from jax.experimental import pallas as pl
from jax.experimental.pallas import tpu as pltpu
from jax.sharding import PartitionSpec as P

BLOCK = 128
HD = 128
GROUP = 4
G = 2
RAND = 3
QB_DEV = 6
NKB = 8
FACTOR = 1.0 / math.sqrt(HD)
EXP_FACTOR = FACTOR * math.log2(math.e)
CONTRACT_LAST = (((1,), (1,)), ((), ()))
CONTRACT_FIRST = (((0,), (0,)), ((), ()))
CONTRACT_MATMUL = (((1,), (0,)), ((), ()))


def dot(a, b, dims=CONTRACT_MATMUL):
    return lax.dot_general(a, b, dims, preferred_element_type=jnp.float32)


def attend_kernel(
    table, valid, query_ref, grad_ref, pool_hbm,
    dquery_ref, local_ref, far_ref, total, scores, dprobs, dscores, keys, held, sems,
):
    step = pl.program_id(0)
    per_dev = local_ref.shape[0]
    entry = [table[step, e] for e in range(NKB)]
    use = [valid[step, e] > 0 for e in range(NKB)]

    @pl.when(step == 0)
    def _():
        load = pltpu.make_async_copy(pool_hbm, held, sems.at[0])
        load.start()
        total[...] = jnp.zeros_like(total)
        load.wait()

    query = jnp.concatenate([query_ref[:, h * HD : (h + 1) * HD] for h in range(GROUP)], axis=0)
    grad = jnp.concatenate([grad_ref[:, h * HD : (h + 1) * HD] for h in range(GROUP)], axis=0)
    rows = [slice(e * BLOCK, (e + 1) * BLOCK) for e in range(NKB)]
    row_max = None
    for e in range(NKB):
        key_tile = held[entry[e], :, :HD]
        keys[rows[e], :] = key_tile
        tile = dot(key_tile, query, CONTRACT_LAST)
        if use[e] is not True:
            tile += jnp.where(use[e], 0.0, -jnp.inf).astype(jnp.float32)
        scores[rows[e], :] = tile
        tile_max = jnp.max(tile, axis=0, keepdims=True)
        row_max = tile_max if e == 0 else jnp.maximum(row_max, tile_max)
    row_sum = jnp.zeros_like(row_max)
    row_dot = jnp.zeros_like(row_max)
    for e in range(NKB):
        weight = jnp.exp2((scores[rows[e], :] - row_max) * EXP_FACTOR)
        dprob = dot(held[entry[e], :, HD:], grad, CONTRACT_LAST)
        row_sum += jnp.sum(weight, axis=0, keepdims=True)
        row_dot += jnp.sum(weight * dprob, axis=0, keepdims=True)
        scores[rows[e], :] = weight
        dprobs[rows[e], :] = dprob
    scale = 1.0 / row_sum
    row_dot = row_dot * scale
    for e in range(NKB):
        weight = scores[rows[e], :] * scale
        dscore = (weight * (dprobs[rows[e], :] - row_dot)).astype(jnp.bfloat16)
        dscores[rows[e], :] = dscore
        total[entry[e], :, :HD] += dot(dscore, query) * FACTOR
        total[entry[e], :, HD:] += dot(weight.astype(jnp.bfloat16), grad)
    dquery = dot(keys[...], dscores[...], CONTRACT_FIRST) * FACTOR
    for h in range(GROUP):
        dquery_ref[:, h * HD : (h + 1) * HD] = dquery[:, h * BLOCK : (h + 1) * BLOCK].T.astype(
            jnp.bfloat16
        )

    @pl.when(step == pl.num_programs(0) - 1)
    def _():
        local_ref[...] = total[:per_dev]
        skip = total.shape[0] - far_ref.shape[0]

        @pl.loop(0, far_ref.shape[0])
        def _(i):
            held[i] = total[skip + i].astype(jnp.bfloat16)
            pltpu.make_async_copy(held.at[i], far_ref.at[i], sems.at[1]).start()

        pltpu.make_async_copy(held.at[pl.ds(0, far_ref.shape[0])], far_ref, sems.at[1]).wait()


def attend(table, valid, queries, grads, pool):
    pool_size = pool.shape[0]
    per_dev = QB_DEV
    far_size = pool_size - per_dev
    anywhere = pl.BlockSpec(memory_space=pl.ANY)
    tile = pl.BlockSpec((BLOCK, GROUP * HD), lambda i, *_: (i, 0))
    whole = lambda size: pl.BlockSpec((size, BLOCK, 2 * HD), lambda i, *_: (0, 0, 0), pipeline_mode=pl.Buffered(1))
    return pl.pallas_call(
        attend_kernel,
        grid_spec=pltpu.PrefetchScalarGridSpec(
            num_scalar_prefetch=2,
            grid=(per_dev,),
            in_specs=[tile, tile, anywhere],
            out_specs=[tile, whole(per_dev), anywhere],
            scratch_shapes=[
                pltpu.VMEM((pool_size, BLOCK, 2 * HD), jnp.float32),
                pltpu.VMEM((NKB * BLOCK, GROUP * BLOCK), jnp.float32),
                pltpu.VMEM((NKB * BLOCK, GROUP * BLOCK), jnp.float32),
                pltpu.VMEM((NKB * BLOCK, GROUP * BLOCK), jnp.bfloat16),
                pltpu.VMEM((NKB * BLOCK, HD), jnp.bfloat16),
                pltpu.VMEM((pool_size, BLOCK, 2 * HD), jnp.bfloat16),
                pltpu.SemaphoreType.DMA((2,)),
            ],
        ),
        out_shape=[
            jax.ShapeDtypeStruct(queries.shape, jnp.bfloat16),
            jax.ShapeDtypeStruct((per_dev, BLOCK, 2 * HD), jnp.float32),
            jax.ShapeDtypeStruct((far_size, BLOCK, 2 * HD), jnp.bfloat16),
        ],
        compiler_params=pltpu.CompilerParams(vmem_limit_bytes=62 << 20),
        name="attend",
    )(table, valid, queries, grads, pool)


def exchange(array):
    return lax.all_to_all(array, "ctx", split_axis=0, concat_axis=0, tiled=True)


def body(queries, keys, values, out_grad, rand_blocks, rand_count):
    heads = lax.axis_size("head")
    shards = lax.axis_size("ctx")
    myself = lax.axis_index("ctx")
    per_dev = QB_DEV
    entries = per_dev * RAND
    owners_used = min(entries, shards - 3)
    capacity = (entries + owners_used - 1) // owners_used
    total_blocks = per_dev * shards
    far_slots = shards * capacity
    piece = G * BLOCK // shards

    tokens = keys.shape[0]
    pairs = jnp.stack([keys.reshape(tokens, heads, HD), values.reshape(tokens, heads, HD)], axis=2)
    pairs = pairs.transpose(1, 0, 2, 3).reshape(heads, tokens, 2 * HD)
    local_rows = lax.all_to_all(pairs, "head", split_axis=0, concat_axis=0, tiled=True)
    local_rows = local_rows.reshape(heads * tokens, 2 * HD)
    local_pairs = local_rows.reshape(per_dev, BLOCK, 2 * HD)
    head_queries = lax.all_to_all(queries, "head", split_axis=1, concat_axis=0, tiled=True)
    head_grads = lax.all_to_all(out_grad, "head", split_axis=1, concat_axis=0, tiled=True)

    flat_blocks = rand_blocks.reshape(shards, entries)
    owners = flat_blocks // per_dev
    offsets = flat_blocks % per_dev
    positions = jnp.arange(entries, dtype=jnp.int32)
    earlier = positions[None, :] < positions[:, None]
    same_owner = owners[:, :, None] == owners[:, None, :]
    slot_ranks = jnp.sum(same_owner & earlier[None], axis=2)
    slot_range = jnp.arange(capacity, dtype=jnp.int32)
    send_hits = (
        (owners == myself)[:, None, :] & (slot_ranks[:, None, :] == slot_range[None, :, None])
    ).astype(jnp.float32)
    offset_hot = (
        offsets[:, :, None] == jnp.arange(per_dev, dtype=jnp.int32)[None, None, :]
    ).astype(jnp.float32)
    send_table = jnp.einsum("dme,deq->dmq", send_hits, offset_hot)
    targets = jnp.arange(shards, dtype=jnp.int32)[:, None, None]
    first_slot = (slot_range == 0)[None, :, None]
    block_range = jnp.arange(per_dev, dtype=jnp.int32)[None, None, :]
    right_send = (targets == (myself + 1) % shards) & first_slot & (block_range == per_dev - 1)
    left_send = (targets == (myself - 1 + shards) % shards) & first_slot & (block_range == 0)
    send_table = send_table + right_send.astype(jnp.float32) + left_send.astype(jnp.float32)
    left_far = per_dev + (myself - 1 + shards) % shards * capacity
    right_far = per_dev + (myself + 1) % shards * capacity
    outgoing = jnp.einsum(
        "dmq,qtc->dmtc",
        send_table.astype(jnp.bfloat16),
        local_pairs,
        preferred_element_type=jnp.float32,
    ).astype(jnp.bfloat16)
    pieces = local_rows[: G * BLOCK].reshape(shards, piece, 2 * HD)
    packed = jnp.concatenate([outgoing.reshape(shards, capacity * BLOCK, 2 * HD), pieces], axis=1)
    arrived = exchange(packed)
    far_pairs = arrived[:, : capacity * BLOCK].reshape(far_slots, BLOCK, 2 * HD)
    my_piece = jnp.broadcast_to(arrived[0, capacity * BLOCK :][None], (shards, piece, 2 * HD))
    global_pairs = exchange(my_piece).reshape(G, BLOCK, 2 * HD)
    pool = jnp.concatenate([local_pairs, far_pairs, global_pairs], axis=0)

    edge_base = per_dev + far_slots
    local_index = jnp.arange(per_dev, dtype=jnp.int32)
    seq_block = myself * per_dev + local_index
    left_index = jnp.where(local_index > 0, local_index - 1, left_far)
    right_index = jnp.where(local_index < per_dev - 1, local_index + 1, right_far)
    global_index = jnp.broadcast_to(
        edge_base + jnp.arange(G, dtype=jnp.int32)[None, :], (per_dev, G)
    )
    my_owners = lax.dynamic_index_in_dim(owners, myself, 0, keepdims=False)
    my_ranks = lax.dynamic_index_in_dim(slot_ranks, myself, 0, keepdims=False)
    random_index = (per_dev + my_owners * capacity + my_ranks).reshape(per_dev, RAND)
    key_table = jnp.concatenate(
        [jnp.stack([left_index, local_index, right_index], axis=1), global_index, random_index],
        axis=1,
    ).astype(jnp.int32)
    my_counts = lax.dynamic_slice_in_dim(rand_count, myself * per_dev, per_dev)
    key_valid = jnp.concatenate(
        [
            jnp.stack([seq_block > 0, seq_block >= 0, seq_block < total_blocks - 1], axis=1),
            jnp.ones((per_dev, G), bool),
            jnp.arange(RAND, dtype=jnp.int32)[None, :] < my_counts[:, None],
        ],
        axis=1,
    ).astype(jnp.int32)

    query_grad, local_grads, far_grads = attend(key_table, key_valid, head_queries, head_grads, pool)

    packed_grads = jnp.concatenate(
        [
            far_grads[:far_slots].reshape(shards, capacity * BLOCK, 2 * HD),
            far_grads[far_slots:].reshape(shards, piece, 2 * HD),
        ],
        axis=1,
    )
    returned = exchange(packed_grads)
    returned_far = returned[:, : capacity * BLOCK].reshape(shards, capacity, BLOCK, 2 * HD)
    global_piece = jnp.sum(returned[:, capacity * BLOCK :].astype(jnp.float32), axis=0)
    global_piece = jnp.broadcast_to(global_piece[None].astype(jnp.bfloat16), (shards, piece, 2 * HD))
    global_total = exchange(global_piece).reshape(G, BLOCK, 2 * HD).astype(jnp.float32)
    local_grads = local_grads + jnp.einsum(
        "dmq,dmtc->qtc",
        send_table.astype(jnp.bfloat16),
        returned_far,
        preferred_element_type=jnp.float32,
    )
    local_grads = local_grads.at[:G].add(
        jnp.where(myself == 0, global_total, jnp.zeros_like(global_total))
    )
    key_grad = local_grads[:, :, :HD].reshape(per_dev * BLOCK, HD).astype(jnp.bfloat16)
    value_grad = local_grads[:, :, HD:].reshape(per_dev * BLOCK, HD).astype(jnp.bfloat16)
    return (query_grad, key_grad, value_grad)


MESH = pl.DeviceIdType.MESH
LINE = 4
SHARD = QB_DEV * BLOCK
ENTRIES = QB_DEV * RAND
CAP = 2
COLUMN = 2 * LINE
DENSE = COLUMN * QB_DEV
SPARSE = COLUMN * CAP
POOL = DENSE + SPARSE + G
HALF = QB_DEV // 2
WINDOW = QB_DEV + 2
WIDE = GROUP * HD
TILE = 16
SPOT, SOURCE, WANTED, GIVEN = 0, 32, 96, 128


def place():
    me = lax.axis_index("ctx")
    return me // 4, (me // 2) % 2, me % 2


def index_of(z, y, c):
    return z * 4 + y * 2 + c


def remote(src, dst, send_sem, recv_sem, **device):
    return pltpu.make_async_remote_copy(
        src_ref=src, dst_ref=dst, send_sem=send_sem, recv_sem=recv_sem, device_id=device, device_id_type=MESH
    )


def greet(z, y, c, head):
    barrier = pltpu.get_barrier_semaphore()

    def tell(**device):
        pl.semaphore_signal(barrier, inc=1, device_id=device, device_id_type=MESH)

    tell(ctx=index_of(z, 1 - y, c))
    tell(ctx=index_of(z, 1 - y, 1 - c))
    tell(ctx=index_of(z, y, 1 - c))
    tell(head=1 - head)

    @pl.when(z > 0)
    def _():
        tell(ctx=index_of(z - 1, y, c))

    @pl.when(z < LINE - 1)
    def _():
        tell(ctx=index_of(z + 1, y, c))

    pl.semaphore_wait(barrier, 4 + (z + 2) // 3 + (5 - z) // 3)


def listed(table, user, owner, missing, by_entry=False):
    first = jnp.int32(missing)
    second = jnp.int32(missing)
    seen = jnp.int32(0)
    for e in range(ENTRIES):
        offset = table[e % RAND, user * QB_DEV + e // RAND] - owner * QB_DEV
        hit = ((offset >= 0) & (offset < QB_DEV)).astype(jnp.int32)
        value = e if by_entry else offset
        second = jnp.where(hit * seen > 0, value, second)
        first = jnp.where(hit * (1 - seen) > 0, value, first)
        seen = jnp.maximum(seen, hit)
    if not by_entry:
        first = jnp.where(user == owner + 1, QB_DEV - 1, first)
        first = jnp.where(user == owner - 1, 0, first)
    return first, second


def stacked(ref, b):
    rows = pl.ds(pl.multiple_of(b * BLOCK, BLOCK), BLOCK)
    return jnp.concatenate([ref[rows, h * HD : (h + 1) * HD] for h in range(GROUP)], axis=0)


def masked(tile, use):
    return tile + jnp.where(use, 0.0, -jnp.inf).astype(jnp.float32)


def column_max(tile):
    return jnp.max(tile, axis=0, keepdims=True)


def column_sum(tile):
    return jnp.sum(tile, axis=0, keepdims=True)


def window_rows(b):
    return pl.ds(pl.multiple_of(b * BLOCK, BLOCK), 3 * BLOCK)


def window_scores(b, block, blocks, queries, grads, window, weights, dprobs, stats):
    query, grad = stacked(queries, b), stacked(grads, b)
    rows = window_rows(b)
    tile = dot(window[0, rows, :], query, CONTRACT_LAST)
    tiles = [tile[i * BLOCK : (i + 1) * BLOCK] for i in range(3)]
    tiles[0] = masked(tiles[0], block > 0)
    tiles[2] = masked(tiles[2], block < blocks - 1)
    top = column_max(jnp.maximum(jnp.maximum(tiles[0], tiles[1]), tiles[2]))
    dprob = dot(window[1, rows, :], grad, CONTRACT_LAST)
    row_sum = jnp.zeros_like(top)
    row_dot = jnp.zeros_like(top)
    for i in range(3):
        part = slice(i * BLOCK, (i + 1) * BLOCK)
        weight = jnp.exp2((tiles[i] - top) * EXP_FACTOR)
        row_sum += column_sum(weight)
        row_dot += column_sum(weight * dprob[part])
        weights[b, part, :] = weight
    dprobs[b] = dprob
    stats[b, 0:1, :] = top
    stats[b, 1:2, :] = row_sum
    stats[b, 2:3, :] = row_dot


def edge_scores(b, queries, grads, edge, weights, dprobs, stats):
    query, grad = stacked(queries, b), stacked(grads, b)
    tile = dot(edge[0], query, CONTRACT_LAST)
    top = column_max(tile)
    dprob = dot(edge[1], grad, CONTRACT_LAST)
    weight = jnp.exp2((tile - top) * EXP_FACTOR)
    weights[b] = weight
    dprobs[b] = dprob
    stats[b, 3:4, :] = top
    stats[b, 4:5, :] = column_sum(weight)
    stats[b, 5:6, :] = column_sum(weight * dprob)


def listed_part(
    b, count, marks, queries, grads, pool, edge_weights, edge_dprobs, stats, dscores, sent, edge_total
):
    query, grad = stacked(queries, b), stacked(grads, b)
    spots = [marks[SPOT + b * RAND + r] for r in range(RAND)]
    window_top, edge_top = stats[b, 0:1, :], stats[b, 3:4, :]
    top = jnp.maximum(window_top, edge_top)
    tiles = []
    for r in range(RAND):
        tile = masked(dot(pool[0, spots[r]], query, CONTRACT_LAST), r < count)
        tiles.append(tile)
        top = jnp.maximum(top, column_max(tile))
    window_part = jnp.exp2((window_top - top) * EXP_FACTOR)
    edge_part = jnp.exp2((edge_top - top) * EXP_FACTOR)
    row_sum = window_part * stats[b, 1:2, :] + edge_part * stats[b, 4:5, :]
    row_dot = window_part * stats[b, 2:3, :] + edge_part * stats[b, 5:6, :]
    weights, dprobs = [], []
    for r in range(RAND):
        weight = jnp.exp2((tiles[r] - top) * EXP_FACTOR)
        dprob = dot(pool[1, spots[r]], grad, CONTRACT_LAST)
        row_sum += column_sum(weight)
        row_dot += column_sum(weight * dprob)
        weights.append(weight)
        dprobs.append(dprob)
    scale = 1.0 / row_sum
    row_dot = row_dot * scale
    for r in range(RAND):
        weight = weights[r] * scale
        dscore = (weight * (dprobs[r] - row_dot)).astype(jnp.bfloat16)
        dscores[b, (5 + r) * BLOCK : (6 + r) * BLOCK, :] = dscore
        sent[0, b * RAND + r] = (dot(dscore, query) * FACTOR).astype(jnp.bfloat16)
        sent[1, b * RAND + r] = dot(weight.astype(jnp.bfloat16), grad).astype(jnp.bfloat16)
    stats[b, 6:7, :] = window_part * scale
    stats[b, 7:8, :] = row_dot
    weight = edge_weights[b] * (edge_part * scale)
    dscore = (weight * (edge_dprobs[b] - row_dot)).astype(jnp.bfloat16)
    dscores[b, 3 * BLOCK : 5 * BLOCK, :] = dscore
    edge_total[0] += dot(dscore, query) * FACTOR
    edge_total[1] += dot(weight.astype(jnp.bfloat16), grad)


def window_part(b, queries, grads, weights, dprobs, stats, dscores, total):
    query, grad = stacked(queries, b), stacked(grads, b)
    weight = weights[b] * stats[b, 6:7, :]
    dscore = (weight * (dprobs[b] - stats[b, 7:8, :])).astype(jnp.bfloat16)
    dscores[b, : 3 * BLOCK, :] = dscore
    rows = window_rows(b)
    total[0, rows, :] += dot(dscore, query) * FACTOR
    total[1, rows, :] += dot(weight.astype(jnp.bfloat16), grad)


def query_part(b, marks, window, edge, pool, dscores, dquery):
    keys = [window[0, window_rows(b), :], edge[0]]
    keys += [pool[0, marks[SPOT + b * RAND + r]] for r in range(RAND)]
    grad = dot(jnp.concatenate(keys, axis=0), dscores[b], CONTRACT_FIRST) * FACTOR
    rows = pl.ds(pl.multiple_of(b * BLOCK, BLOCK), BLOCK)
    for h in range(GROUP):
        dquery[rows, h * HD : (h + 1) * HD] = grad[:, h * BLOCK : (h + 1) * BLOCK].T.astype(jnp.bfloat16)


def line_kernel(
    table, count, q_in, k_in, v_in, g_in, query_grad, key_grad, value_grad,
    marks, queries, grads, pool, packed, window, edge, stats,
    window_weights, window_dprobs, edge_weights, edge_dprobs, dscores,
    sent, outbox, total, edge_total, edge_out, edge_in, edge_sum, beside_in, across_in, z_out, z_in, dquery,
    local_sem, head_send, head_recv, up_send, down_send, gz_recv, gy_send, gy_recv, gc_send, gc_recv,
    ge_send, ge_recv, rc_send, rc_recv, ry_send, ry_recv, re_send, re_recv, rz_send, rz_recv, out_sem,
):
    z, y, c = place()
    me = index_of(z, y, c)
    head = lax.axis_index("head")
    other = 1 - head
    tokens = q_in.shape[0]
    blocks = table.shape[1]
    first_block = me * QB_DEV

    def line_of(zz, cc):
        return (zz * 2 + cc) * QB_DEV

    token_rows = pl.ds(pl.multiple_of(head * tokens, tokens), tokens)
    arrivals = pl.ds(line_of(z, c) + head * HALF, HALF)

    def lane(side, width):
        return pl.ds(pl.multiple_of(side * width, width), width)

    jobs = []
    for src, dst, width in (
        (k_in, pool.at[0, arrivals], HD),
        (v_in, pool.at[1, arrivals], HD),
        (q_in, queries.at[token_rows, :], WIDE),
        (g_in, grads.at[token_rows, :], WIDE),
    ):
        i = len(jobs)
        if i < 2:
            mine, theirs = src.at[:, :, lane(head, width)], src.at[:, :, lane(other, width)]
        else:
            mine, theirs = src.at[:, lane(head, width)], src.at[:, lane(other, width)]
        jobs.append(
            (
                pltpu.make_async_copy(mine, dst, local_sem.at[i]),
                remote(theirs, dst, head_send.at[i], head_recv.at[i], head=other),
            )
        )
    for local, _ in jobs:
        local.start()
    greet(z, y, c, head)
    for _, away in jobs[:2]:
        away.start()

    def quarter(zz, u, kv):
        return pool.at[kv, pl.ds(line_of(zz, c) + u * HALF, HALF)], (zz * 2 + u) * 2 + kv

    def up(zz, u, kv):
        part, i = quarter(zz, u, kv)
        return remote(part, part, up_send.at[i], gz_recv.at[i], ctx=index_of((z + 1) % LINE, y, c))

    def down(zz, u, kv):
        part, i = quarter(zz, u, kv)
        return remote(part, part, down_send.at[i], gz_recv.at[i], ctx=index_of((z + 3) % LINE, y, c))

    def beside(zz, kv):
        part = pool.at[kv, pl.ds(line_of(zz, c), QB_DEV)]
        i = zz * 2 + kv
        return remote(part, part, gc_send.at[i], gc_recv.at[i], ctx=index_of(z, y, 1 - c))

    def across(zz, kv, d, sender):
        slots = pool.at[kv, pl.ds(DENSE + (zz * 2 + sender) * CAP, CAP)]
        i = zz * 2 + kv
        return remote(packed.at[zz, kv, d], slots, gy_send.at[d, i], gy_recv.at[sender, i], ctx=index_of(z, 1 - y, d))

    def edge_across(kv, d):
        return remote(
            pool.at[kv, :G], pool.at[kv, DENSE + SPARSE :], ge_send.at[d, kv], ge_recv.at[kv], ctx=index_of(z, 1 - y, d)
        )

    def complete(zz, kv):
        wanted = [marks[WANTED + zz * 4 + s] for s in range(2 * CAP)]
        line = line_of(zz, c)

        @pl.loop(0, BLOCK // TILE)
        def _(i):
            rows = pl.ds(pl.multiple_of(i * TILE, TILE), TILE)
            tiles = [pool[kv, line + q, rows, :] for q in range(QB_DEV)]
            for s, want in enumerate(wanted):
                tile = tiles[0]
                for q in range(1, QB_DEV):
                    tile = jnp.where(want == q, tiles[q], tile)
                packed[zz, kv, s // CAP, s % CAP, rows, :] = tile

        for d in range(2):
            across(zz, kv, d, c).start()
        beside(zz, kv).start()

        @pl.when((zz == 0) & (y == 0) & (c == 0))
        def _():
            for d in range(2):
                edge_across(kv, d).start()

    def pass_on(zz, u, kv, upward, downward):
        if upward:

            @pl.when(z < LINE - 1)
            def _():
                up(zz, u, kv).start()

        if downward:

            @pl.when(z > 0)
            def _():
                down(zz, u, kv).start()

    for kv in range(2):
        jobs[kv][0].wait()
        pass_on(z, head, kv, True, True)

    @pl.loop(0, LINE)
    def _(zz):
        for d in range(2):
            pair = listed(table, index_of(z, 1 - y, d), index_of(zz, y, c), 0)
            for k in range(CAP):
                marks[WANTED + zz * 4 + d * CAP + k] = pair[k]

    for kv in range(2):
        jobs[kv][1].wait_recv()
        pass_on(z, other, kv, True, True)
        complete(z, kv)
    for _, away in jobs[2:]:
        away.start()

    def stage(j):
        for u in (head, other):
            for kv in range(2):

                @pl.when(z - j >= 0)
                def _():
                    up(z - j, u, kv).wait_recv()
                    pass_on(z - j, u, kv, True, False)

                @pl.when(z + j <= LINE - 1)
                def _():
                    down(z + j, u, kv).wait_recv()
                    pass_on(z + j, u, kv, False, True)

                if u is other:

                    @pl.when(z - j >= 0)
                    def _():
                        complete(z - j, kv)

                    @pl.when(z + j <= LINE - 1)
                    def _():
                        complete(z + j, kv)

    stage(1)

    owners = []
    for e in range(ENTRIES):
        named = table[e % RAND, first_block + e // RAND]
        owner = named // QB_DEV
        rank = jnp.int32(0)
        for before in owners:
            rank += (before == owner).astype(jnp.int32)
        owners.append(owner)
        line = (owner // 4) * 2 + owner % 2
        same = (owner // 2) % 2 == y
        marks[SPOT + e] = jnp.where(same, line * QB_DEV + named - owner * QB_DEV, DENSE + line * CAP + rank)

    @pl.loop(0, 4 * LINE)
    def _(owner):
        pair = listed(table, me, owner, 0, by_entry=True)
        for k in range(CAP):
            marks[SOURCE + owner * CAP + k] = pair[k]

    @pl.loop(0, LINE)
    def _(zz):
        users = (me, index_of(z, y, 1 - c), index_of(z, 1 - y, 0), index_of(z, 1 - y, 1))
        for i, user in enumerate(users):
            pair = listed(table, user, index_of(zz, y, c), -1)
            for k in range(CAP):
                marks[GIVEN + zz * 8 + i * CAP + k] = pair[k]

    stage(2)

    for local, away in jobs[2:]:
        local.wait()
        away.wait_recv()
    for kv in range(2):
        beside(z, kv).wait_recv()
    near = z + jnp.where(c == 0, y - 1, y)
    has_near = (near >= 0) & (near < LINE)

    @pl.when(has_near)
    def _():
        for kv in range(2):
            across(near, kv, 0, 1 - c).wait_recv()

    near_slot = DENSE + (near * 2 + 1 - c) * CAP
    mine = line_of(z, c)
    left = jnp.where(c == 1, line_of(z, 0) + QB_DEV - 1, jnp.where(has_near, near_slot, mine))
    right = jnp.where(c == 0, line_of(z, 1), jnp.where(has_near, near_slot, mine))
    for kv in range(2):
        window[kv, :BLOCK, :] = pool[kv, left]
        for q in range(QB_DEV):
            window[kv, (q + 1) * BLOCK : (q + 2) * BLOCK, :] = pool[kv, mine + q]
        window[kv, (WINDOW - 1) * BLOCK :, :] = pool[kv, right]

    @pl.loop(0, QB_DEV)
    def _(b):
        window_scores(
            b, first_block + b, blocks, queries, grads, window, window_weights, window_dprobs, stats
        )

    total[...] = jnp.zeros_like(total)
    edge_total[...] = jnp.zeros_like(edge_total)
    edge_sum[...] = jnp.zeros_like(edge_sum)
    stage(3)

    for zz in range(LINE):

        @pl.when(zz != z)
        def _():
            for kv in range(2):
                beside(zz, kv).wait_recv()

    @pl.when(y == 1)
    def _():
        for kv in range(2):
            edge_across(kv, 0).wait_recv()

    edge_spot = jnp.where(y == 0, 0, DENSE + SPARSE)
    for kv in range(2):
        for g in range(G):
            edge[kv, g * BLOCK : (g + 1) * BLOCK, :] = pool[kv, edge_spot + g]

    @pl.loop(0, QB_DEV)
    def _(b):
        edge_scores(b, queries, grads, edge, edge_weights, edge_dprobs, stats)

    for zz in range(LINE):
        for sender in range(2):

            @pl.when((zz != near) | (sender == c))
            def _():
                for kv in range(2):
                    across(zz, kv, 0, sender).wait_recv()

    @pl.loop(0, QB_DEV)
    def _(b):
        listed_part(
            b, count[first_block + b], marks, queries, grads, pool, edge_weights, edge_dprobs, stats, dscores,
            sent, edge_total,
        )

    def window_sums(b):
        window_part(b, queries, grads, window_weights, window_dprobs, stats, dscores, total)

    @pl.loop(0, 2)
    def _(i):
        window_sums(i * (QB_DEV - 1))

    @pl.loop(0, 4 * LINE * CAP)
    def _(s):
        for kv in range(2):
            outbox[kv, s] = sent[kv, marks[SOURCE + s]]

    @pl.when(me > 0)
    def _():
        for kv in range(2):
            outbox[kv, (me - 1) * CAP] = total[kv, :BLOCK, :].astype(jnp.bfloat16)

    @pl.when(me < 4 * LINE - 1)
    def _():
        for kv in range(2):
            outbox[kv, (me + 1) * CAP] = total[kv, (WINDOW - 1) * BLOCK :, :].astype(jnp.bfloat16)

    edge_out[...] = edge_total[...].astype(jnp.bfloat16)

    def out_slots(zz, yy, cc, kv):
        return outbox.at[kv, pl.ds(index_of(zz, yy, cc) * CAP, CAP)]

    def give_beside(zz, kv):
        i = zz * 2 + kv
        return remote(
            out_slots(zz, y, 1 - c, kv), beside_in.at[zz, kv], rc_send.at[i], rc_recv.at[i], ctx=index_of(z, y, 1 - c)
        )

    def give_across(zz, kv, d, sender):
        i = zz * 2 + kv
        return remote(
            out_slots(zz, 1 - y, d, kv), across_in.at[sender, zz, kv],
            ry_send.at[d, i], ry_recv.at[sender, i], ctx=index_of(z, 1 - y, d),
        )

    def give_edge(kind, **device):
        return remote(edge_out, edge_in.at[kind], re_send.at[0], re_recv.at[kind], **device)

    def give_up(zz, kv):
        i = zz * 2 + kv
        return remote(
            z_out.at[zz, kv], z_in.at[0, zz, kv], rz_send.at[i], rz_recv.at[0, i], ctx=index_of((z + 1) % LINE, y, c)
        )

    def give_down(zz, kv):
        i = zz * 2 + kv
        return remote(
            z_out.at[zz, kv], z_in.at[1, zz, kv], rz_send.at[i], rz_recv.at[1, i], ctx=index_of((z + 3) % LINE, y, c)
        )

    def pick(options):
        return jnp.where(z == 0, options[0], jnp.where(z == 1, options[1], jnp.where(z == 2, options[2], options[3])))

    order = [pick(options) for options in ((3, 3, 0, 0), (2, 0, 3, 1), (1, 2, 1, 2))] + [z]
    units = [(zz, kv) for zz in order for kv in range(2)]
    holder = (y == 0) & (c == 0)
    corner = index_of(z, 0, 0)

    @pl.when((y == 0) & (c == 1))
    def _():
        give_edge(1, ctx=corner).start()

    for d in range(2):

        @pl.when((y == 1) & (c == d))
        def _():
            give_edge(2 + d, ctx=corner).start()

    for zz, kv in units:
        for d in range(2):
            give_across(zz, kv, d, c).start()
        give_beside(zz, kv).start()

    @pl.loop(1, QB_DEV - 1)
    def _(b):
        window_sums(b)

    def keep_query(b):
        rows = pl.ds(pl.multiple_of(b * BLOCK, BLOCK), BLOCK)
        return pltpu.make_async_copy(dquery.at[rows, :], query_grad.at[rows, :], out_sem.at[b])

    def take(i):
        zz, kv = units[i]
        last = i >= len(units) - 2
        give_beside(zz, kv).wait_recv()
        for d in range(2):
            give_across(zz, kv, 0, d).wait_recv()
        wanted = [marks[GIVEN + zz * 8 + s] for s in range(4 * CAP)]
        slots = index_of(zz, y, c) * CAP
        at_edge = holder & (zz == 0)
        if kv == 0:

            @pl.when(at_edge)
            def _():
                for kind in range(1, 4):
                    give_edge(kind, ctx=index_of(z, 0, 1)).wait_recv()
                sums = edge_total[...]
                for kind in range(1, 4):
                    sums += edge_in[kind].astype(jnp.float32)
                edge_sum[...] = sums

        def add(sides):
            @pl.loop(0, BLOCK // TILE)
            def _(t):
                row = pl.multiple_of(t * TILE, TILE)
                tile_rows = pl.ds(row, TILE)
                tiles = [outbox[kv, slots + k, tile_rows, :] for k in range(CAP)]
                for ref in (beside_in.at[zz, kv], across_in.at[0, zz, kv], across_in.at[1, zz, kv]):
                    tiles += [ref[k, tile_rows, :] for k in range(CAP)]
                tiles = [tile.astype(jnp.float32) for tile in tiles]
                for q in range(QB_DEV):
                    rows = pl.ds(pl.multiple_of(q * BLOCK + row, TILE), TILE)
                    sums = None
                    if last:
                        sums = total[kv, pl.ds(pl.multiple_of((q + 1) * BLOCK + row, TILE), TILE), :]
                    for side in sides:
                        part = z_in[side, zz, kv, rows, :].astype(jnp.float32)
                        sums = part if sums is None else sums + part
                    for want, tile in zip(wanted, tiles):
                        part = jnp.where(want == q, tile, 0.0)
                        sums = part if sums is None else sums + part
                    if q < G:
                        sums += jnp.where(at_edge, edge_sum[kv, rows, :], 0.0)
                    sums = sums.astype(jnp.bfloat16)
                    if last and kv == 0:
                        key_grad[rows, :] = sums
                    elif last:
                        value_grad[rows, :] = sums
                    else:
                        z_out[zz, kv, rows, :] = sums

        if last:

            @pl.when(z == 0)
            def _():
                give_down(zz, kv).wait_recv()
                add((1,))

            @pl.when(z == LINE - 1)
            def _():
                give_up(zz, kv).wait_recv()
                add((0,))

            @pl.when((z > 0) & (z < LINE - 1))
            def _():
                give_up(zz, kv).wait_recv()
                give_down(zz, kv).wait_recv()
                add((0, 1))

            return

        @pl.when((z == 0) | (z == LINE - 1))
        def _():
            add(())

        @pl.when((z > 0) & (z < LINE - 1) & (zz > z))
        def _():
            give_up(zz, kv).wait_recv()
            add((0,))

        @pl.when((z > 0) & (z < LINE - 1) & (zz < z))
        def _():
            give_down(zz, kv).wait_recv()
            add((1,))

        @pl.when(zz > z)
        def _():
            give_up(zz, kv).start()

        @pl.when(zz < z)
        def _():
            give_down(zz, kv).start()

    for i in range(len(units)):
        take(i)
        if i < QB_DEV:
            query_part(i, marks, window, edge, pool, dscores, dquery)
            keep_query(i).start()

    for i, (zz, kv) in enumerate(units):
        give_beside(zz, kv).wait_send()
        for d in range(2):
            give_across(zz, kv, d, c).wait_send()
        if i < len(units) - 2:
            give_up(zz, kv).wait_send()

    @pl.when((y == 1) | (c == 1))
    def _():
        give_edge(1, ctx=index_of(z, 1 - y, c)).wait_send()

    for zz in range(LINE):
        for kv in range(2):
            beside(zz, kv).wait_send()
            for d in range(2):
                across(zz, kv, d, c).wait_send()
            for u in range(2):

                @pl.when((z < LINE - 1) & (zz <= z))
                def _():
                    up(zz, u, kv).wait_send()

                @pl.when((z > 0) & (zz >= z))
                def _():
                    down(zz, u, kv).wait_send()

    @pl.when(holder)
    def _():
        for kv in range(2):
            for d in range(2):
                edge_across(kv, d).wait_send()

    for _, away in jobs:
        away.wait_send()
    for b in range(QB_DEV):
        keep_query(b).wait()


def body_line(queries, keys, values, out_grad, rand_blocks, rand_count):
    anywhere = pl.BlockSpec(memory_space=pl.ANY)
    scalars = pl.BlockSpec(memory_space=pltpu.SMEM)
    in_vmem = pl.BlockSpec(memory_space=pltpu.VMEM)
    dma = pltpu.SemaphoreType.DMA
    bf16, f32 = jnp.bfloat16, jnp.float32
    keys = keys.reshape(HALF, BLOCK, 2 * HD)
    values = values.reshape(HALF, BLOCK, 2 * HD)
    result = jax.ShapeDtypeStruct((SHARD, HD), bf16)
    pair = 2 * LINE
    return pl.pallas_call(
        line_kernel,
        in_specs=[scalars, scalars] + [anywhere] * 4,
        out_specs=[anywhere, in_vmem, in_vmem],
        out_shape=[jax.ShapeDtypeStruct((SHARD, WIDE), bf16), result, result],
        scratch_shapes=[
            pltpu.SMEM((192,), jnp.int32),
            pltpu.VMEM((SHARD, WIDE), bf16),
            pltpu.VMEM((SHARD, WIDE), bf16),
            pltpu.VMEM((2, POOL, BLOCK, HD), bf16),
            pltpu.VMEM((LINE, 2, 2, CAP, BLOCK, HD), bf16),
            pltpu.VMEM((2, WINDOW * BLOCK, HD), bf16),
            pltpu.VMEM((2, G * BLOCK, HD), bf16),
            pltpu.VMEM((QB_DEV, 8, WIDE), f32),
            pltpu.VMEM((QB_DEV, 3 * BLOCK, WIDE), f32),
            pltpu.VMEM((QB_DEV, 3 * BLOCK, WIDE), f32),
            pltpu.VMEM((QB_DEV, G * BLOCK, WIDE), f32),
            pltpu.VMEM((QB_DEV, G * BLOCK, WIDE), f32),
            pltpu.VMEM((QB_DEV, NKB * BLOCK, WIDE), bf16),
            pltpu.VMEM((2, ENTRIES, BLOCK, HD), bf16),
            pltpu.VMEM((2, 4 * LINE * CAP, BLOCK, HD), bf16),
            pltpu.VMEM((2, WINDOW * BLOCK, HD), f32),
            pltpu.VMEM((2, G * BLOCK, HD), f32),
            pltpu.VMEM((2, G * BLOCK, HD), bf16),
            pltpu.VMEM((4, 2, G * BLOCK, HD), bf16),
            pltpu.VMEM((2, G * BLOCK, HD), f32),
            pltpu.VMEM((LINE, 2, CAP, BLOCK, HD), bf16),
            pltpu.VMEM((2, LINE, 2, CAP, BLOCK, HD), bf16),
            pltpu.VMEM((LINE, 2, SHARD, HD), bf16),
            pltpu.VMEM((2, LINE, 2, SHARD, HD), bf16),
            pltpu.VMEM((SHARD, WIDE), bf16),
            dma((4,)), dma((4,)), dma((4,)), dma((2 * pair,)), dma((2 * pair,)), dma((2 * pair,)),
            dma((2, pair)), dma((2, pair)), dma((pair,)), dma((pair,)), dma((2, 2)), dma((2,)),
            dma((pair,)), dma((pair,)), dma((2, pair)), dma((2, pair)), dma((1,)), dma((4,)),
            dma((pair,)), dma((2, pair)), dma((QB_DEV,)),
        ],
        compiler_params=pltpu.CompilerParams(
            collective_id=0, has_side_effects=True, vmem_limit_bytes=62 << 20
        ),
        name="line",
    )(rand_blocks.T, rand_count, queries, keys, values, out_grad)


def solution(mesh):
    line = mesh.shape["ctx"] == 4 * LINE and mesh.shape["head"] == 2
    placed = P(("ctx", "head"), None)
    return jax.shard_map(
        body_line if line else body,
        mesh=mesh,
        in_specs=(placed, placed, placed, placed, P(), P()),
        out_specs=(P("ctx", "head"), P("ctx", "head"), P("ctx", "head")),
        check_vma=False,
    )
```

```python
import math

import jax
import jax.numpy as jnp
from jax import lax
from jax.experimental import pallas as pl
from jax.experimental.pallas import tpu as pltpu
from jax.sharding import PartitionSpec as P

BLOCK = 128
HD = 128
GROUP = 4
G = 2
RAND = 3
QB_DEV = 6
NKB = 8
FACTOR = 1.0 / math.sqrt(HD)
EXP_FACTOR = FACTOR * math.log2(math.e)
CONTRACT_LAST = (((1,), (1,)), ((), ()))
CONTRACT_FIRST = (((0,), (0,)), ((), ()))
CONTRACT_MATMUL = (((1,), (0,)), ((), ()))


def dot(a, b, dims=CONTRACT_MATMUL):
    return lax.dot_general(a, b, dims, preferred_element_type=jnp.float32)


def attend_kernel(
    table, valid, query_ref, grad_ref, pool_hbm,
    dquery_ref, local_ref, far_ref, total, scores, dprobs, dscores, keys, held, sems,
):
    step = pl.program_id(0)
    per_dev = local_ref.shape[0]
    entry = [table[step, e] for e in range(NKB)]
    use = [valid[step, e] > 0 for e in range(NKB)]

    @pl.when(step == 0)
    def _():
        load = pltpu.make_async_copy(pool_hbm, held, sems.at[0])
        load.start()
        total[...] = jnp.zeros_like(total)
        load.wait()

    query = jnp.concatenate([query_ref[:, h * HD : (h + 1) * HD] for h in range(GROUP)], axis=0)
    grad = jnp.concatenate([grad_ref[:, h * HD : (h + 1) * HD] for h in range(GROUP)], axis=0)
    rows = [slice(e * BLOCK, (e + 1) * BLOCK) for e in range(NKB)]
    row_max = None
    for e in range(NKB):
        key_tile = held[entry[e], :, :HD]
        keys[rows[e], :] = key_tile
        tile = dot(key_tile, query, CONTRACT_LAST)
        if use[e] is not True:
            tile += jnp.where(use[e], 0.0, -jnp.inf).astype(jnp.float32)
        scores[rows[e], :] = tile
        tile_max = jnp.max(tile, axis=0, keepdims=True)
        row_max = tile_max if e == 0 else jnp.maximum(row_max, tile_max)
    row_sum = jnp.zeros_like(row_max)
    row_dot = jnp.zeros_like(row_max)
    for e in range(NKB):
        weight = jnp.exp2((scores[rows[e], :] - row_max) * EXP_FACTOR)
        dprob = dot(held[entry[e], :, HD:], grad, CONTRACT_LAST)
        row_sum += jnp.sum(weight, axis=0, keepdims=True)
        row_dot += jnp.sum(weight * dprob, axis=0, keepdims=True)
        scores[rows[e], :] = weight
        dprobs[rows[e], :] = dprob
    scale = 1.0 / row_sum
    row_dot = row_dot * scale
    for e in range(NKB):
        weight = scores[rows[e], :] * scale
        dscore = (weight * (dprobs[rows[e], :] - row_dot)).astype(jnp.bfloat16)
        dscores[rows[e], :] = dscore
        total[entry[e], :, :HD] += dot(dscore, query) * FACTOR
        total[entry[e], :, HD:] += dot(weight.astype(jnp.bfloat16), grad)
    dquery = dot(keys[...], dscores[...], CONTRACT_FIRST) * FACTOR
    for h in range(GROUP):
        dquery_ref[:, h * HD : (h + 1) * HD] = dquery[:, h * BLOCK : (h + 1) * BLOCK].T.astype(
            jnp.bfloat16
        )

    @pl.when(step == pl.num_programs(0) - 1)
    def _():
        local_ref[...] = total[:per_dev]
        skip = total.shape[0] - far_ref.shape[0]

        @pl.loop(0, far_ref.shape[0])
        def _(i):
            held[i] = total[skip + i].astype(jnp.bfloat16)
            pltpu.make_async_copy(held.at[i], far_ref.at[i], sems.at[1]).start()

        pltpu.make_async_copy(held.at[pl.ds(0, far_ref.shape[0])], far_ref, sems.at[1]).wait()


def attend(table, valid, queries, grads, pool):
    pool_size = pool.shape[0]
    per_dev = QB_DEV
    far_size = pool_size - per_dev
    anywhere = pl.BlockSpec(memory_space=pl.ANY)
    tile = pl.BlockSpec((BLOCK, GROUP * HD), lambda i, *_: (i, 0))
    whole = lambda size: pl.BlockSpec((size, BLOCK, 2 * HD), lambda i, *_: (0, 0, 0), pipeline_mode=pl.Buffered(1))
    return pl.pallas_call(
        attend_kernel,
        grid_spec=pltpu.PrefetchScalarGridSpec(
            num_scalar_prefetch=2,
            grid=(per_dev,),
            in_specs=[tile, tile, anywhere],
            out_specs=[tile, whole(per_dev), anywhere],
            scratch_shapes=[
                pltpu.VMEM((pool_size, BLOCK, 2 * HD), jnp.float32),
                pltpu.VMEM((NKB * BLOCK, GROUP * BLOCK), jnp.float32),
                pltpu.VMEM((NKB * BLOCK, GROUP * BLOCK), jnp.float32),
                pltpu.VMEM((NKB * BLOCK, GROUP * BLOCK), jnp.bfloat16),
                pltpu.VMEM((NKB * BLOCK, HD), jnp.bfloat16),
                pltpu.VMEM((pool_size, BLOCK, 2 * HD), jnp.bfloat16),
                pltpu.SemaphoreType.DMA((2,)),
            ],
        ),
        out_shape=[
            jax.ShapeDtypeStruct(queries.shape, jnp.bfloat16),
            jax.ShapeDtypeStruct((per_dev, BLOCK, 2 * HD), jnp.float32),
            jax.ShapeDtypeStruct((far_size, BLOCK, 2 * HD), jnp.bfloat16),
        ],
        compiler_params=pltpu.CompilerParams(vmem_limit_bytes=62 << 20),
        name="attend",
    )(table, valid, queries, grads, pool)


def exchange(array):
    return lax.all_to_all(array, "ctx", split_axis=0, concat_axis=0, tiled=True)


def body(queries, keys, values, out_grad, rand_blocks, rand_count):
    heads = lax.axis_size("head")
    shards = lax.axis_size("ctx")
    myself = lax.axis_index("ctx")
    per_dev = QB_DEV
    entries = per_dev * RAND
    owners_used = min(entries, shards - 3)
    capacity = (entries + owners_used - 1) // owners_used
    total_blocks = per_dev * shards
    far_slots = shards * capacity
    piece = G * BLOCK // shards

    tokens = keys.shape[0]
    pairs = jnp.stack([keys.reshape(tokens, heads, HD), values.reshape(tokens, heads, HD)], axis=2)
    pairs = pairs.transpose(1, 0, 2, 3).reshape(heads, tokens, 2 * HD)
    local_rows = lax.all_to_all(pairs, "head", split_axis=0, concat_axis=0, tiled=True)
    local_rows = local_rows.reshape(heads * tokens, 2 * HD)
    local_pairs = local_rows.reshape(per_dev, BLOCK, 2 * HD)
    head_queries = lax.all_to_all(queries, "head", split_axis=1, concat_axis=0, tiled=True)
    head_grads = lax.all_to_all(out_grad, "head", split_axis=1, concat_axis=0, tiled=True)

    flat_blocks = rand_blocks.reshape(shards, entries)
    owners = flat_blocks // per_dev
    offsets = flat_blocks % per_dev
    positions = jnp.arange(entries, dtype=jnp.int32)
    earlier = positions[None, :] < positions[:, None]
    same_owner = owners[:, :, None] == owners[:, None, :]
    slot_ranks = jnp.sum(same_owner & earlier[None], axis=2)
    slot_range = jnp.arange(capacity, dtype=jnp.int32)
    send_hits = (
        (owners == myself)[:, None, :] & (slot_ranks[:, None, :] == slot_range[None, :, None])
    ).astype(jnp.float32)
    offset_hot = (
        offsets[:, :, None] == jnp.arange(per_dev, dtype=jnp.int32)[None, None, :]
    ).astype(jnp.float32)
    send_table = jnp.einsum("dme,deq->dmq", send_hits, offset_hot)
    targets = jnp.arange(shards, dtype=jnp.int32)[:, None, None]
    first_slot = (slot_range == 0)[None, :, None]
    block_range = jnp.arange(per_dev, dtype=jnp.int32)[None, None, :]
    right_send = (targets == (myself + 1) % shards) & first_slot & (block_range == per_dev - 1)
    left_send = (targets == (myself - 1 + shards) % shards) & first_slot & (block_range == 0)
    send_table = send_table + right_send.astype(jnp.float32) + left_send.astype(jnp.float32)
    left_far = per_dev + (myself - 1 + shards) % shards * capacity
    right_far = per_dev + (myself + 1) % shards * capacity
    outgoing = jnp.einsum(
        "dmq,qtc->dmtc",
        send_table.astype(jnp.bfloat16),
        local_pairs,
        preferred_element_type=jnp.float32,
    ).astype(jnp.bfloat16)
    pieces = local_rows[: G * BLOCK].reshape(shards, piece, 2 * HD)
    packed = jnp.concatenate([outgoing.reshape(shards, capacity * BLOCK, 2 * HD), pieces], axis=1)
    arrived = exchange(packed)
    far_pairs = arrived[:, : capacity * BLOCK].reshape(far_slots, BLOCK, 2 * HD)
    my_piece = jnp.broadcast_to(arrived[0, capacity * BLOCK :][None], (shards, piece, 2 * HD))
    global_pairs = exchange(my_piece).reshape(G, BLOCK, 2 * HD)
    pool = jnp.concatenate([local_pairs, far_pairs, global_pairs], axis=0)

    edge_base = per_dev + far_slots
    local_index = jnp.arange(per_dev, dtype=jnp.int32)
    seq_block = myself * per_dev + local_index
    left_index = jnp.where(local_index > 0, local_index - 1, left_far)
    right_index = jnp.where(local_index < per_dev - 1, local_index + 1, right_far)
    global_index = jnp.broadcast_to(
        edge_base + jnp.arange(G, dtype=jnp.int32)[None, :], (per_dev, G)
    )
    my_owners = lax.dynamic_index_in_dim(owners, myself, 0, keepdims=False)
    my_ranks = lax.dynamic_index_in_dim(slot_ranks, myself, 0, keepdims=False)
    random_index = (per_dev + my_owners * capacity + my_ranks).reshape(per_dev, RAND)
    key_table = jnp.concatenate(
        [jnp.stack([left_index, local_index, right_index], axis=1), global_index, random_index],
        axis=1,
    ).astype(jnp.int32)
    my_counts = lax.dynamic_slice_in_dim(rand_count, myself * per_dev, per_dev)
    key_valid = jnp.concatenate(
        [
            jnp.stack([seq_block > 0, seq_block >= 0, seq_block < total_blocks - 1], axis=1),
            jnp.ones((per_dev, G), bool),
            jnp.arange(RAND, dtype=jnp.int32)[None, :] < my_counts[:, None],
        ],
        axis=1,
    ).astype(jnp.int32)

    query_grad, local_grads, far_grads = attend(key_table, key_valid, head_queries, head_grads, pool)

    packed_grads = jnp.concatenate(
        [
            far_grads[:far_slots].reshape(shards, capacity * BLOCK, 2 * HD),
            far_grads[far_slots:].reshape(shards, piece, 2 * HD),
        ],
        axis=1,
    )
    returned = exchange(packed_grads)
    returned_far = returned[:, : capacity * BLOCK].reshape(shards, capacity, BLOCK, 2 * HD)
    global_piece = jnp.sum(returned[:, capacity * BLOCK :].astype(jnp.float32), axis=0)
    global_piece = jnp.broadcast_to(global_piece[None].astype(jnp.bfloat16), (shards, piece, 2 * HD))
    global_total = exchange(global_piece).reshape(G, BLOCK, 2 * HD).astype(jnp.float32)
    local_grads = local_grads + jnp.einsum(
        "dmq,dmtc->qtc",
        send_table.astype(jnp.bfloat16),
        returned_far,
        preferred_element_type=jnp.float32,
    )
    local_grads = local_grads.at[:G].add(
        jnp.where(myself == 0, global_total, jnp.zeros_like(global_total))
    )
    key_grad = local_grads[:, :, :HD].reshape(per_dev * BLOCK, HD).astype(jnp.bfloat16)
    value_grad = local_grads[:, :, HD:].reshape(per_dev * BLOCK, HD).astype(jnp.bfloat16)
    return (query_grad, key_grad, value_grad)


MESH = pl.DeviceIdType.MESH
LINE = 4
SHARD = QB_DEV * BLOCK
ENTRIES = QB_DEV * RAND
CAP = 2
COLUMN = 2 * LINE
DENSE = COLUMN * QB_DEV
SPARSE = COLUMN * CAP
POOL = DENSE + SPARSE + G
HALF = QB_DEV // 2
WINDOW = QB_DEV + 2
WIDE = GROUP * HD
TILE = 16
SPOT, SOURCE, WANTED, GIVEN = 0, 32, 96, 128


def place():
    me = lax.axis_index("ctx")
    return me // 4, (me // 2) % 2, me % 2


def index_of(z, y, c):
    return z * 4 + y * 2 + c


def remote(src, dst, send_sem, recv_sem, **device):
    return pltpu.make_async_remote_copy(
        src_ref=src, dst_ref=dst, send_sem=send_sem, recv_sem=recv_sem, device_id=device, device_id_type=MESH
    )


def greet(z, y, c, head):
    barrier = pltpu.get_barrier_semaphore()

    def tell(**device):
        pl.semaphore_signal(barrier, inc=1, device_id=device, device_id_type=MESH)

    tell(ctx=index_of(z, 1 - y, c))
    tell(ctx=index_of(z, 1 - y, 1 - c))
    tell(ctx=index_of(z, y, 1 - c))
    tell(head=1 - head)

    @pl.when(z > 0)
    def _():
        tell(ctx=index_of(z - 1, y, c))

    @pl.when(z < LINE - 1)
    def _():
        tell(ctx=index_of(z + 1, y, c))

    pl.semaphore_wait(barrier, 4 + (z + 2) // 3 + (5 - z) // 3)


def listed(table, user, owner, missing, by_entry=False):
    first = jnp.int32(missing)
    second = jnp.int32(missing)
    seen = jnp.int32(0)
    for e in range(ENTRIES):
        offset = table[e % RAND, user * QB_DEV + e // RAND] - owner * QB_DEV
        hit = ((offset >= 0) & (offset < QB_DEV)).astype(jnp.int32)
        value = e if by_entry else offset
        second = jnp.where(hit * seen > 0, value, second)
        first = jnp.where(hit * (1 - seen) > 0, value, first)
        seen = jnp.maximum(seen, hit)
    if not by_entry:
        first = jnp.where(user == owner + 1, QB_DEV - 1, first)
        first = jnp.where(user == owner - 1, 0, first)
    return first, second


def stacked(ref, b):
    rows = pl.ds(pl.multiple_of(b * BLOCK, BLOCK), BLOCK)
    return jnp.concatenate([ref[rows, h * HD : (h + 1) * HD] for h in range(GROUP)], axis=0)


def masked(tile, use):
    return tile + jnp.where(use, 0.0, -jnp.inf).astype(jnp.float32)


def column_max(tile):
    return jnp.max(tile, axis=0, keepdims=True)


def column_sum(tile):
    return jnp.sum(tile, axis=0, keepdims=True)


def window_rows(b):
    return pl.ds(pl.multiple_of(b * BLOCK, BLOCK), 3 * BLOCK)


TOP_W, SUM_W, TOP_E, SUM_E, SCALE_W, SCALE_E, PART, DOT = (slice(i, i + 1) for i in range(8))


def window_scores(b, block, blocks, queries, window, weights, stats):
    tile = dot(window[0, window_rows(b), :], stacked(queries, b), CONTRACT_LAST)
    tiles = [tile[i * BLOCK : (i + 1) * BLOCK] for i in range(3)]
    tiles[0] = masked(tiles[0], block > 0)
    tiles[2] = masked(tiles[2], block < blocks - 1)
    top = column_max(jnp.maximum(jnp.maximum(tiles[0], tiles[1]), tiles[2]))
    row_sum = jnp.zeros_like(top)
    for i in range(3):
        weight = jnp.exp2((tiles[i] - top) * EXP_FACTOR)
        row_sum += column_sum(weight)
        weights[b, i * BLOCK : (i + 1) * BLOCK, :] = weight
    stats[b, TOP_W, :] = top
    stats[b, SUM_W, :] = row_sum


def edge_scores(b, queries, edge, weights, stats):
    tile = dot(edge[0], stacked(queries, b), CONTRACT_LAST)
    top = column_max(tile)
    weight = jnp.exp2((tile - top) * EXP_FACTOR)
    weights[b] = weight
    stats[b, TOP_E, :] = top
    stats[b, SUM_E, :] = column_sum(weight)


def listed_scores(b, count, marks, queries, grads, keys, weights, stats, sent):
    query, grad = stacked(queries, b), stacked(grads, b)
    window_top, edge_top = stats[b, TOP_W, :], stats[b, TOP_E, :]
    top = jnp.maximum(window_top, edge_top)
    tiles = []
    for r in range(RAND):
        tile = masked(dot(keys[marks[SPOT + b * RAND + r]], query, CONTRACT_LAST), r < count)
        tiles.append(tile)
        top = jnp.maximum(top, column_max(tile))
    window_part = jnp.exp2((window_top - top) * EXP_FACTOR)
    edge_part = jnp.exp2((edge_top - top) * EXP_FACTOR)
    row_sum = window_part * stats[b, SUM_W, :] + edge_part * stats[b, SUM_E, :]
    for r in range(RAND):
        tiles[r] = jnp.exp2((tiles[r] - top) * EXP_FACTOR)
        row_sum += column_sum(tiles[r])
    scale = 1.0 / row_sum
    stats[b, SCALE_W, :] = window_part * scale
    stats[b, SCALE_E, :] = edge_part * scale
    for r in range(RAND):
        weight = tiles[r] * scale
        weights[b, r * BLOCK : (r + 1) * BLOCK, :] = weight
        sent[1, b * RAND + r] = dot(weight.astype(jnp.bfloat16), grad).astype(jnp.bfloat16)


def edge_values(b, grads, weights, stats, edge_total):
    weight = weights[b] * stats[b, SCALE_E, :]
    edge_total[1] += dot(weight.astype(jnp.bfloat16), stacked(grads, b))


def window_values(b, grads, weights, stats, total):
    weight = weights[b] * stats[b, SCALE_W, :]
    total[1, window_rows(b), :] += dot(weight.astype(jnp.bfloat16), stacked(grads, b))


def window_dots(b, grads, window, weights, dprobs, stats):
    dprob = dot(window[1, window_rows(b), :], stacked(grads, b), CONTRACT_LAST)
    dprobs[b] = dprob
    stats[b, PART, :] = column_sum(weights[b] * dprob) * stats[b, SCALE_W, :]


def edge_dots(b, grads, edge, weights, dprobs, stats):
    dprob = dot(edge[1], stacked(grads, b), CONTRACT_LAST)
    dprobs[b] = dprob
    stats[b, PART, :] += column_sum(weights[b] * dprob) * stats[b, SCALE_E, :]


def listed_dots(b, marks, queries, grads, values, weights, stats, dscores, sent):
    query, grad = stacked(queries, b), stacked(grads, b)
    row_dot = stats[b, PART, :]
    dprobs = []
    for r in range(RAND):
        dprob = dot(values[marks[SPOT + b * RAND + r]], grad, CONTRACT_LAST)
        row_dot += column_sum(weights[b, r * BLOCK : (r + 1) * BLOCK, :] * dprob)
        dprobs.append(dprob)
    stats[b, DOT, :] = row_dot
    for r in range(RAND):
        weight = weights[b, r * BLOCK : (r + 1) * BLOCK, :]
        dscore = (weight * (dprobs[r] - row_dot)).astype(jnp.bfloat16)
        dscores[b, (5 + r) * BLOCK : (6 + r) * BLOCK, :] = dscore
        sent[0, b * RAND + r] = (dot(dscore, query) * FACTOR).astype(jnp.bfloat16)


def edge_keys(b, queries, weights, dprobs, stats, dscores, edge_total):
    weight = weights[b] * stats[b, SCALE_E, :]
    dscore = (weight * (dprobs[b] - stats[b, DOT, :])).astype(jnp.bfloat16)
    dscores[b, 3 * BLOCK : 5 * BLOCK, :] = dscore
    edge_total[0] += dot(dscore, stacked(queries, b)) * FACTOR


def window_keys(b, queries, weights, dprobs, stats, dscores, total):
    weight = weights[b] * stats[b, SCALE_W, :]
    dscore = (weight * (dprobs[b] - stats[b, DOT, :])).astype(jnp.bfloat16)
    dscores[b, : 3 * BLOCK, :] = dscore
    total[0, window_rows(b), :] += dot(dscore, stacked(queries, b)) * FACTOR


def query_part(b, marks, window, edge, listed_keys, dscores, dquery):
    keys = [window[0, window_rows(b), :], edge[0]]
    keys += [listed_keys[marks[SPOT + b * RAND + r]] for r in range(RAND)]
    grad = dot(jnp.concatenate(keys, axis=0), dscores[b], CONTRACT_FIRST) * FACTOR
    rows = pl.ds(pl.multiple_of(b * BLOCK, BLOCK), BLOCK)
    for h in range(GROUP):
        dquery[rows, h * HD : (h + 1) * HD] = grad[:, h * BLOCK : (h + 1) * BLOCK].T.astype(jnp.bfloat16)


def line_kernel(
    table, count, q_in, k_in, v_in, g_in, query_grad, key_grad, value_grad,
    marks, queries, grads, key_pool, value_pool, staged, packed, window, edge, stats,
    window_weights, window_dprobs, edge_weights, edge_dprobs, listed_weights, dscores,
    sent, outbox, total, edge_total, edge_out, edge_in, edge_sum, beside_in, across_in, z_out, z_in, dquery, dpair,
    local_sem, stage_sem, head_send, head_recv, up_send, down_send, gz_recv, gy_send, gy_recv, gc_send, gc_recv,
    ge_send, ge_recv, rc_send, rc_recv, ry_send, ry_recv, re_send, re_recv, rz_send, rz_recv, out_sem,
):
    z, y, c = place()
    me = index_of(z, y, c)
    head = lax.axis_index("head")
    other = 1 - head
    tokens = q_in.shape[0]
    blocks = table.shape[1]
    first_block = me * QB_DEV
    pools = (key_pool, value_pool)

    def line_of(zz, cc):
        return (zz * 2 + cc) * QB_DEV

    token_rows = pl.ds(pl.multiple_of(head * tokens, tokens), tokens)
    arrivals = pl.ds(line_of(z, c) + head * HALF, HALF)

    def lane(side, width):
        return pl.ds(pl.multiple_of(side * width, width), width)

    def keep_pair(kv):
        src = (k_in, v_in)[kv].at[:, :, lane(head, HD)]
        return pltpu.make_async_copy(src, pools[kv].at[arrivals], local_sem.at[kv])

    def stage_pair(kv):
        src = (k_in, v_in)[kv].at[:, :, lane(other, HD)]
        return pltpu.make_async_copy(src, staged.at[kv], stage_sem.at[kv])

    def swap_pair(kv):
        return remote(staged.at[kv], pools[kv].at[arrivals], head_send.at[kv], head_recv.at[kv], head=other)

    def keep_wide(i):
        src, dst = ((q_in, queries), (g_in, grads))[i]
        return pltpu.make_async_copy(src.at[:, lane(head, WIDE)], dst.at[token_rows, :], local_sem.at[2 + i])

    def swap_wide(i):
        src, dst = ((q_in, queries), (g_in, grads))[i]
        return remote(
            src.at[:, lane(other, WIDE)], dst.at[token_rows, :], head_send.at[2 + i], head_recv.at[2 + i], head=other
        )

    for kv in range(2):
        keep_pair(kv).start()
        stage_pair(kv).start()
    for i in range(2):
        keep_wide(i).start()
    greet(z, y, c, head)
    for kv in range(2):
        stage_pair(kv).wait()
        swap_pair(kv).start()

    def quarter(zz, u, kv):
        return pools[kv].at[pl.ds(line_of(zz, c) + u * HALF, HALF)], (zz * 2 + u) * 2 + kv

    def up(zz, u, kv):
        part, i = quarter(zz, u, kv)
        return remote(part, part, up_send.at[i], gz_recv.at[i], ctx=index_of((z + 1) % LINE, y, c))

    def down(zz, u, kv):
        part, i = quarter(zz, u, kv)
        return remote(part, part, down_send.at[i], gz_recv.at[i], ctx=index_of((z + 3) % LINE, y, c))

    def beside(zz, kv):
        part = pools[kv].at[pl.ds(line_of(zz, c), QB_DEV)]
        i = zz * 2 + kv
        return remote(part, part, gc_send.at[i], gc_recv.at[i], ctx=index_of(z, y, 1 - c))

    def across(zz, kv, d, sender):
        slots = pools[kv].at[pl.ds(DENSE + (zz * 2 + sender) * CAP, CAP)]
        i = zz * 2 + kv
        return remote(packed.at[zz, kv, d], slots, gy_send.at[d, i], gy_recv.at[sender, i], ctx=index_of(z, 1 - y, d))

    edge_slots = pl.ds(DENSE + SPARSE, G)

    def edge_across(kv):
        return remote(
            pools[kv].at[pl.ds(0, G)], pools[kv].at[edge_slots], ge_send.at[kv], ge_recv.at[kv],
            ctx=index_of(z, 1 - y, 0),
        )

    def edge_beside(kv):
        part = pools[kv].at[edge_slots]
        return remote(part, part, ge_send.at[kv], ge_recv.at[kv], ctx=index_of(z, y, 1 - c))

    first_edge = (y == 0) & (c == 0)

    def complete(zz, kv):
        @pl.when((zz == 0) & first_edge)
        def _():
            edge_across(kv).start()

        wanted = [marks[WANTED + zz * 4 + s] for s in range(2 * CAP)]
        line = line_of(zz, c)

        @pl.loop(0, BLOCK // TILE)
        def _(i):
            rows = pl.ds(pl.multiple_of(i * TILE, TILE), TILE)
            tiles = [pools[kv][line + q, rows, :] for q in range(QB_DEV)]
            for s, want in enumerate(wanted):
                tile = tiles[0]
                for q in range(1, QB_DEV):
                    tile = jnp.where(want == q, tiles[q], tile)
                packed[zz, kv, s // CAP, s % CAP, rows, :] = tile

        for d in range(2):
            across(zz, kv, d, c).start()
        beside(zz, kv).start()

    def pass_on(zz, u, kv, upward, downward):
        if upward:

            @pl.when(z < LINE - 1)
            def _():
                up(zz, u, kv).start()

        if downward:

            @pl.when(z > 0)
            def _():
                down(zz, u, kv).start()

    def hop(j, u, kv):
        @pl.when(z - j >= 0)
        def _():
            up(z - j, u, kv).wait_recv()
            pass_on(z - j, u, kv, True, False)

        @pl.when(z + j <= LINE - 1)
        def _():
            down(z + j, u, kv).wait_recv()
            pass_on(z + j, u, kv, False, True)

    def done(j, kv):
        @pl.when(z - j >= 0)
        def _():
            complete(z - j, kv)

        @pl.when(z + j <= LINE - 1)
        def _():
            complete(z + j, kv)

    for kv in range(2):
        keep_pair(kv).wait()
        pass_on(z, head, kv, True, True)
    @pl.loop(0, LINE)
    def _(zz):
        for d in range(2):
            pair = listed(table, index_of(z, 1 - y, d), index_of(zz, y, c), 0)
            for k in range(CAP):
                marks[WANTED + zz * 4 + d * CAP + k] = pair[k]

    swap_pair(0).wait_recv()
    pass_on(z, other, 0, True, True)
    swap_wide(0).start()
    hop(1, head, 0)
    complete(z, 0)
    swap_pair(1).wait_recv()
    pass_on(z, other, 1, True, True)
    swap_wide(1).start()
    complete(z, 1)
    hop(1, other, 0)
    done(1, 0)
    hop(1, head, 1)
    hop(1, other, 1)
    done(1, 1)

    owners = []
    for e in range(ENTRIES):
        named = table[e % RAND, first_block + e // RAND]
        owner = named // QB_DEV
        rank = jnp.int32(0)
        for before in owners:
            rank += (before == owner).astype(jnp.int32)
        owners.append(owner)
        line = (owner // 4) * 2 + owner % 2
        same = (owner // 2) % 2 == y
        marks[SPOT + e] = jnp.where(same, line * QB_DEV + named - owner * QB_DEV, DENSE + line * CAP + rank)

    @pl.loop(0, 4 * LINE)
    def _(owner):
        pair = listed(table, me, owner, 0, by_entry=True)
        for k in range(CAP):
            marks[SOURCE + owner * CAP + k] = pair[k]

    @pl.loop(0, LINE)
    def _(zz):
        users = (me, index_of(z, y, 1 - c), index_of(z, 1 - y, 0), index_of(z, 1 - y, 1))
        for i, user in enumerate(users):
            pair = listed(table, user, index_of(zz, y, c), -1)
            for k in range(CAP):
                marks[GIVEN + zz * 8 + i * CAP + k] = pair[k]

    hop(2, head, 0)
    hop(2, other, 0)
    done(2, 0)
    hop(2, head, 1)
    hop(2, other, 1)
    done(2, 1)

    near = z + jnp.where(c == 0, y - 1, y)
    has_near = (near >= 0) & (near < LINE)
    near_slot = DENSE + (near * 2 + 1 - c) * CAP
    mine = line_of(z, c)
    left = jnp.where(c == 1, line_of(z, 0) + QB_DEV - 1, jnp.where(has_near, near_slot, mine))
    right = jnp.where(c == 0, line_of(z, 1), jnp.where(has_near, near_slot, mine))

    def fill_window(kv):
        beside(z, kv).wait_recv()

        @pl.when(has_near)
        def _():
            across(near, kv, 0, 1 - c).wait_recv()

        window[kv, :BLOCK, :] = pools[kv][left]
        for q in range(QB_DEV):
            window[kv, (q + 1) * BLOCK : (q + 2) * BLOCK, :] = pools[kv][mine + q]
        window[kv, (WINDOW - 1) * BLOCK :, :] = pools[kv][right]

    def fill_edge(kv):
        for zz in range(LINE):

            @pl.when(zz != z)
            def _():
                beside(zz, kv).wait_recv()

        @pl.when(y == 1)
        def _():
            edge_across(kv).wait_recv()

        @pl.when((y == 1) & (c == 0))
        def _():
            edge_beside(kv).start()

        spot = jnp.where(y == 0, 0, DENSE + SPARSE)
        for g in range(G):
            edge[kv, g * BLOCK : (g + 1) * BLOCK, :] = pools[kv][spot + g]

    def slots_arrived(kv):
        for zz in range(LINE):
            for sender in range(2):

                @pl.when((zz != near) | (sender == c))
                def _():
                    across(zz, kv, 0, sender).wait_recv()

    total[...] = jnp.zeros_like(total)
    edge_total[...] = jnp.zeros_like(edge_total)
    edge_sum[...] = jnp.zeros_like(edge_sum)
    hop(3, head, 0)
    hop(3, other, 0)
    done(3, 0)
    fill_window(0)
    keep_wide(0).wait()
    swap_wide(0).wait_recv()

    @pl.loop(0, QB_DEV)
    def _(b):
        window_scores(b, first_block + b, blocks, queries, window, window_weights, stats)

    fill_edge(0)

    @pl.loop(0, QB_DEV)
    def _(b):
        edge_scores(b, queries, edge, edge_weights, stats)

    hop(3, head, 1)
    hop(3, other, 1)
    done(3, 1)
    slots_arrived(0)
    keep_wide(1).wait()
    swap_wide(1).wait_recv()

    @pl.loop(0, QB_DEV, unroll=2)
    def _(b):
        listed_scores(
            b, count[first_block + b], marks, queries, grads, key_pool, listed_weights, stats, sent
        )

    def window_value_sums(b):
        window_values(b, grads, window_weights, stats, total)

    def window_key_sums(b):
        window_keys(b, queries, window_weights, window_dprobs, stats, dscores, total)

    def fill_outbox(kv):
        @pl.loop(0, 4 * LINE * CAP)
        def _(s):
            outbox[kv, s] = sent[kv, marks[SOURCE + s]]

    def fill_near(kv):
        @pl.when(me > 0)
        def _():
            outbox[kv, (me - 1) * CAP] = total[kv, :BLOCK, :].astype(jnp.bfloat16)

        @pl.when(me < 4 * LINE - 1)
        def _():
            outbox[kv, (me + 1) * CAP] = total[kv, (WINDOW - 1) * BLOCK :, :].astype(jnp.bfloat16)

    def out_slots(zz, yy, cc, kv):
        return outbox.at[kv, pl.ds(index_of(zz, yy, cc) * CAP, CAP)]

    def give_beside(zz, kv):
        i = zz * 2 + kv
        return remote(
            out_slots(zz, y, 1 - c, kv), beside_in.at[zz, kv], rc_send.at[i], rc_recv.at[i], ctx=index_of(z, y, 1 - c)
        )

    def give_across(zz, kv, d, sender):
        i = zz * 2 + kv
        return remote(
            out_slots(zz, 1 - y, d, kv), across_in.at[sender, zz, kv],
            ry_send.at[d, i], ry_recv.at[sender, i], ctx=index_of(z, 1 - y, d),
        )

    def give_edge_beside(kv):
        return remote(
            edge_out.at[kv], edge_in.at[0, kv], re_send.at[kv], re_recv.at[0, kv], ctx=index_of(z, y, 1 - c)
        )

    def give_edge_across(kv):
        return remote(
            edge_out.at[kv], edge_in.at[1, kv], re_send.at[kv], re_recv.at[1, kv], ctx=index_of(z, 1 - y, c)
        )

    def half_unit(zz, kv, half):
        return pl.ds(pl.multiple_of(half * (SHARD // 2), SHARD // 2), SHARD // 2), (zz * 2 + kv) * 2 + half

    def give_up(zz, kv, half):
        rows, i = half_unit(zz, kv, half)
        return remote(
            z_out.at[zz, kv, rows, :], z_in.at[0, zz, kv, rows, :], rz_send.at[i], rz_recv.at[0, i],
            ctx=index_of((z + 1) % LINE, y, c),
        )

    def give_down(zz, kv, half):
        rows, i = half_unit(zz, kv, half)
        return remote(
            z_out.at[zz, kv, rows, :], z_in.at[1, zz, kv, rows, :], rz_send.at[i], rz_recv.at[1, i],
            ctx=index_of((z + 3) % LINE, y, c),
        )

    def pick(options):
        return jnp.where(z == 0, options[0], jnp.where(z == 1, options[1], jnp.where(z == 2, options[2], options[3])))

    order = [pick(options) for options in ((3, 3, 0, 0), (2, 0, 3, 1), (1, 2, 1, 2))] + [z]

    def give(i, kv):
        for d in range(2):
            give_across(order[i], kv, d, c).start()
        give_beside(order[i], kv).start()

    def give_edges(kv):
        @pl.when(c == 1)
        def _():
            edge_out[kv] = edge_total[kv].astype(jnp.bfloat16)
            give_edge_beside(kv).start()

    def sum_edges(kv):
        @pl.when(c == 0)
        def _():
            give_edge_beside(kv).wait_recv()
            edge_sum[kv] = edge_total[kv] + edge_in[0, kv].astype(jnp.float32)

        @pl.when((c == 0) & (y == 1))
        def _():
            edge_out[kv] = edge_sum[kv].astype(jnp.bfloat16)
            give_edge_across(kv).start()

    def take(i, kv, before=None):
        zz = order[i]
        before = None if before is None else (order[before[0]], before[1])
        last = i == LINE - 1
        give_beside(zz, kv).wait_recv()
        for d in range(2):
            give_across(zz, kv, 0, d).wait_recv()
        wanted = [marks[GIVEN + zz * 8 + s] for s in range(4 * CAP)]
        slots = index_of(zz, y, c) * CAP
        at_edge = first_edge & (zz == 0)

        below = (zz >= z if last else zz > z) & (z > 0)
        above = (zz <= z if last else zz < z) & (z < LINE - 1)

        @pl.loop(0, 2)
        def _(turn):
            half = 1 - turn

            @pl.when(at_edge & (half == 0))
            def _():
                give_edge_across(kv).wait_recv()
                edge_sum[kv] += edge_in[1, kv].astype(jnp.float32)

            @pl.when(below)
            def _():
                give_up(zz, kv, half).wait_recv()

            @pl.when(above)
            def _():
                give_down(zz, kv, half).wait_recv()

            @pl.loop(0, BLOCK // TILE)
            def _(t):
                row = pl.multiple_of(t * TILE, TILE)
                tile_rows = pl.ds(row, TILE)
                tiles = [outbox[kv, slots + k, tile_rows, :] for k in range(CAP)]
                for ref in (beside_in.at[zz, kv], across_in.at[0, zz, kv], across_in.at[1, zz, kv]):
                    tiles += [ref[k, tile_rows, :] for k in range(CAP)]
                tiles = [tile.astype(jnp.float32) for tile in tiles]
                for i in range(HALF):
                    q = half * HALF + i
                    rows = pl.ds(pl.multiple_of(q * BLOCK + row, TILE), TILE)
                    sums = jnp.where(below, z_in[0, zz, kv, rows, :].astype(jnp.float32), 0.0)
                    sums += jnp.where(above, z_in[1, zz, kv, rows, :].astype(jnp.float32), 0.0)
                    if last:
                        sums += total[kv, pl.ds(pl.multiple_of((q + 1) * BLOCK + row, TILE), TILE), :]
                    for want, tile in zip(wanted, tiles):
                        sums += jnp.where(want == q, tile, 0.0)
                    if i < G:
                        edge_rows = pl.ds(pl.multiple_of(i * BLOCK + row, TILE), TILE)
                        sums += jnp.where(at_edge & (half == 0), edge_sum[kv, edge_rows, :], 0.0)
                    sums = sums.astype(jnp.bfloat16)
                    if last:
                        dpair[kv, rows, :] = sums
                    else:
                        z_out[zz, kv, rows, :] = sums

            if not last:
                if before is not None:
                    give_up(*before, half).wait_send()

                @pl.when(zz > z)
                def _():
                    give_up(zz, kv, half).start()

                @pl.when(zz < z)
                def _():
                    give_down(zz, kv, half).start()

    def query_sums(b):
        query_part(b, marks, window, edge, key_pool, dscores, dquery)
        keep_query(b).start()

    def keep_query(b):
        rows = pl.ds(pl.multiple_of(b * BLOCK, BLOCK), BLOCK)
        return pltpu.make_async_copy(dquery.at[rows, :], query_grad.at[rows, :], out_sem.at[b])

    def keep_result(kv):
        return pltpu.make_async_copy(dpair.at[kv], (key_grad, value_grad)[kv], out_sem.at[QB_DEV + kv])

    at_end = (z == 0) | (z == LINE - 1)

    fill_outbox(1)
    give(0, 1)

    @pl.loop(0, QB_DEV)
    def _(b):
        edge_values(b, grads, edge_weights, stats, edge_total)

    give_edges(1)

    @pl.loop(0, QB_DEV)
    def _(b):
        window_value_sums(b)

    fill_near(1)
    sum_edges(1)
    give(1, 1)
    fill_window(1)

    @pl.loop(0, QB_DEV)
    def _(b):
        window_dots(b, grads, window, window_weights, window_dprobs, stats)

    fill_edge(1)

    @pl.loop(0, QB_DEV)
    def _(b):
        edge_dots(b, grads, edge, edge_weights, edge_dprobs, stats)

    @pl.when(at_end)
    def _():
        take(0, 1)

    give(2, 1)
    slots_arrived(1)

    @pl.loop(0, QB_DEV, unroll=2)
    def _(b):
        listed_dots(b, marks, queries, grads, value_pool, listed_weights, stats, dscores, sent)

    fill_outbox(0)
    give(0, 0)

    def edge_key_sums():
        @pl.loop(0, QB_DEV)
        def _(b):
            edge_keys(b, queries, edge_weights, edge_dprobs, stats, dscores, edge_total)

        give_edges(0)

    @pl.when(jnp.logical_not(at_end))
    def _():
        edge_key_sums()
        take(0, 1)

    take(1, 1)

    @pl.when(at_end)
    def _():
        edge_key_sums()

    @pl.loop(0, QB_DEV)
    def _(b):
        window_key_sums(b)

    fill_near(0)
    sum_edges(0)
    give(1, 0)
    query_sums(0)
    take(2, 1, (0, 1))
    query_sums(1)
    query_sums(2)
    give(2, 0)
    take(0, 0, (1, 1))
    query_sums(3)
    give(3, 1)
    query_sums(4)
    take(1, 0, (2, 1))
    give(3, 0)
    query_sums(5)
    take(2, 0, (0, 0))
    take(3, 1)
    keep_result(1).start()
    take(3, 0)
    keep_result(0).start()

    for half in range(2):
        give_up(order[2], 0, half).wait_send()
        give_up(order[1], 0, half).wait_send()
    for zz in range(LINE):
        for kv in range(2):
            beside(zz, kv).wait_send()
            give_beside(zz, kv).wait_send()
            for d in range(2):
                across(zz, kv, d, c).wait_send()
                give_across(zz, kv, d, c).wait_send()

            for u in range(2):

                @pl.when((z < LINE - 1) & (zz <= z))
                def _():
                    up(zz, u, kv).wait_send()

                @pl.when((z > 0) & (zz >= z))
                def _():
                    down(zz, u, kv).wait_send()

    for kv in range(2):

        @pl.when(c == 1)
        def _():
            give_edge_beside(kv).wait_send()

        @pl.when((c == 0) & (y == 1))
        def _():
            give_edge_across(kv).wait_send()
            edge_beside(kv).wait_send()

        @pl.when(first_edge)
        def _():
            edge_across(kv).wait_send()

        swap_wide(kv).wait_send()
        swap_pair(kv).wait_send()
    for b in range(QB_DEV):
        keep_query(b).wait()
    for kv in range(2):
        keep_result(kv).wait()


def settle_kernel(*refs):
    sources, targets, held, in_sem, out_sem = refs[:3], refs[3:6], refs[6:9], refs[9], refs[10]
    copies = []
    for src, dst, mid in zip(sources, targets, held):
        step = 2 * BLOCK
        for i in range(src.shape[0] // step):
            rows, n = pl.ds(i * step, step), len(copies)
            copies.append(
                (
                    pltpu.make_async_copy(src.at[rows, :], mid.at[rows, :], in_sem.at[n]),
                    pltpu.make_async_copy(mid.at[rows, :], dst.at[rows, :], out_sem.at[n]),
                )
            )
    for arrive, _ in copies:
        arrive.start()
    for arrive, leave in copies:
        arrive.wait()
        leave.start()
    for _, leave in copies:
        leave.wait()


def settle(arrays):
    anywhere = pl.BlockSpec(memory_space=pl.ANY)
    dma = pltpu.SemaphoreType.DMA
    return pl.pallas_call(
        settle_kernel,
        in_specs=[anywhere] * 3,
        out_specs=[anywhere] * 3,
        out_shape=[jax.ShapeDtypeStruct(array.shape, array.dtype) for array in arrays],
        scratch_shapes=[pltpu.VMEM(array.shape, array.dtype) for array in arrays] + [dma((9,)), dma((9,))],
        compiler_params=pltpu.CompilerParams(vmem_limit_bytes=62 << 20),
        name="settle",
    )(*arrays)


def body_line(queries, keys, values, out_grad, rand_blocks, rand_count):
    anywhere = pl.BlockSpec(memory_space=pl.ANY)
    scalars = pl.BlockSpec(memory_space=pltpu.SMEM)
    dma = pltpu.SemaphoreType.DMA
    bf16, f32 = jnp.bfloat16, jnp.float32
    keys = keys.reshape(HALF, BLOCK, 2 * HD)
    values = values.reshape(HALF, BLOCK, 2 * HD)
    result = jax.ShapeDtypeStruct((SHARD, HD), bf16)
    pair = 2 * LINE
    grads = pl.pallas_call(
        line_kernel,
        in_specs=[scalars, scalars] + [anywhere] * 4,
        out_specs=[anywhere] * 3,
        out_shape=[jax.ShapeDtypeStruct((SHARD, WIDE), bf16), result, result],
        scratch_shapes=[
            pltpu.SMEM((192,), jnp.int32),
            pltpu.VMEM((SHARD, WIDE), bf16),
            pltpu.VMEM((SHARD, WIDE), bf16),
            pltpu.VMEM((POOL, BLOCK, HD), bf16),
            pltpu.VMEM((POOL, BLOCK, HD), bf16),
            pltpu.VMEM((2, HALF, BLOCK, HD), bf16),
            pltpu.VMEM((LINE, 2, 2, CAP, BLOCK, HD), bf16),
            pltpu.VMEM((2, WINDOW * BLOCK, HD), bf16),
            pltpu.VMEM((2, G * BLOCK, HD), bf16),
            pltpu.VMEM((QB_DEV, 8, WIDE), f32),
            pltpu.VMEM((QB_DEV, 3 * BLOCK, WIDE), f32),
            pltpu.VMEM((QB_DEV, 3 * BLOCK, WIDE), f32),
            pltpu.VMEM((QB_DEV, G * BLOCK, WIDE), f32),
            pltpu.VMEM((QB_DEV, G * BLOCK, WIDE), f32),
            pltpu.VMEM((QB_DEV, RAND * BLOCK, WIDE), f32),
            pltpu.VMEM((QB_DEV, NKB * BLOCK, WIDE), bf16),
            pltpu.VMEM((2, ENTRIES, BLOCK, HD), bf16),
            pltpu.VMEM((2, 4 * LINE * CAP, BLOCK, HD), bf16),
            pltpu.VMEM((2, WINDOW * BLOCK, HD), f32),
            pltpu.VMEM((2, G * BLOCK, HD), f32),
            pltpu.VMEM((2, G * BLOCK, HD), bf16),
            pltpu.VMEM((2, 2, G * BLOCK, HD), bf16),
            pltpu.VMEM((2, G * BLOCK, HD), f32),
            pltpu.VMEM((LINE, 2, CAP, BLOCK, HD), bf16),
            pltpu.VMEM((2, LINE, 2, CAP, BLOCK, HD), bf16),
            pltpu.VMEM((LINE, 2, SHARD, HD), bf16),
            pltpu.VMEM((2, LINE, 2, SHARD, HD), bf16),
            pltpu.VMEM((SHARD, WIDE), bf16),
            pltpu.VMEM((2, SHARD, HD), bf16),
            dma((4,)), dma((2,)), dma((4,)), dma((4,)), dma((2 * pair,)), dma((2 * pair,)), dma((2 * pair,)),
            dma((2, pair)), dma((2, pair)), dma((pair,)), dma((pair,)), dma((2,)), dma((2,)),
            dma((pair,)), dma((pair,)), dma((2, pair)), dma((2, pair)), dma((2,)), dma((2, 2)),
            dma((2 * pair,)), dma((2, 2 * pair)), dma((QB_DEV + 2,)),
        ],
        compiler_params=pltpu.CompilerParams(
            collective_id=0, has_side_effects=True, vmem_limit_bytes=62 << 20
        ),
        name="line",
    )(rand_blocks.T, rand_count, queries, keys, values, out_grad)
    return tuple(settle(grads))


def solution(mesh):
    line = mesh.shape["ctx"] == 4 * LINE and mesh.shape["head"] == 2
    placed = P(("ctx", "head"), None)
    return jax.shard_map(
        body_line if line else body,
        mesh=mesh,
        in_specs=(placed, placed, placed, placed, P(), P()),
        out_specs=(P("ctx", "head"), P("ctx", "head"), P("ctx", "head")),
        check_vma=False,
    )
```

```python
import math

import jax
import jax.numpy as jnp
from jax import lax
from jax.experimental import pallas as pl
from jax.experimental.pallas import tpu as pltpu
from jax.sharding import PartitionSpec as P

BLOCK = 128
HD = 128
GROUP = 4
G = 2
RAND = 3
QB_DEV = 6
NKB = 8
FACTOR = 1.0 / math.sqrt(HD)
EXP_FACTOR = FACTOR * math.log2(math.e)
CONTRACT_LAST = (((1,), (1,)), ((), ()))
CONTRACT_FIRST = (((0,), (0,)), ((), ()))
CONTRACT_MATMUL = (((1,), (0,)), ((), ()))


def dot(a, b, dims=CONTRACT_MATMUL):
    return lax.dot_general(a, b, dims, preferred_element_type=jnp.float32)


def attend_kernel(
    table, valid, query_ref, grad_ref, pool_hbm,
    dquery_ref, local_ref, far_ref, total, scores, dprobs, dscores, keys, held, sems,
):
    step = pl.program_id(0)
    per_dev = local_ref.shape[0]
    entry = [table[step, e] for e in range(NKB)]
    use = [valid[step, e] > 0 for e in range(NKB)]

    @pl.when(step == 0)
    def _():
        load = pltpu.make_async_copy(pool_hbm, held, sems.at[0])
        load.start()
        total[...] = jnp.zeros_like(total)
        load.wait()

    query = jnp.concatenate([query_ref[:, h * HD : (h + 1) * HD] for h in range(GROUP)], axis=0)
    grad = jnp.concatenate([grad_ref[:, h * HD : (h + 1) * HD] for h in range(GROUP)], axis=0)
    rows = [slice(e * BLOCK, (e + 1) * BLOCK) for e in range(NKB)]
    row_max = None
    for e in range(NKB):
        key_tile = held[entry[e], :, :HD]
        keys[rows[e], :] = key_tile
        tile = dot(key_tile, query, CONTRACT_LAST)
        if use[e] is not True:
            tile += jnp.where(use[e], 0.0, -jnp.inf).astype(jnp.float32)
        scores[rows[e], :] = tile
        tile_max = jnp.max(tile, axis=0, keepdims=True)
        row_max = tile_max if e == 0 else jnp.maximum(row_max, tile_max)
    row_sum = jnp.zeros_like(row_max)
    row_dot = jnp.zeros_like(row_max)
    for e in range(NKB):
        weight = jnp.exp2((scores[rows[e], :] - row_max) * EXP_FACTOR)
        dprob = dot(held[entry[e], :, HD:], grad, CONTRACT_LAST)
        row_sum += jnp.sum(weight, axis=0, keepdims=True)
        row_dot += jnp.sum(weight * dprob, axis=0, keepdims=True)
        scores[rows[e], :] = weight
        dprobs[rows[e], :] = dprob
    scale = 1.0 / row_sum
    row_dot = row_dot * scale
    for e in range(NKB):
        weight = scores[rows[e], :] * scale
        dscore = (weight * (dprobs[rows[e], :] - row_dot)).astype(jnp.bfloat16)
        dscores[rows[e], :] = dscore
        total[entry[e], :, :HD] += dot(dscore, query) * FACTOR
        total[entry[e], :, HD:] += dot(weight.astype(jnp.bfloat16), grad)
    dquery = dot(keys[...], dscores[...], CONTRACT_FIRST) * FACTOR
    for h in range(GROUP):
        dquery_ref[:, h * HD : (h + 1) * HD] = dquery[:, h * BLOCK : (h + 1) * BLOCK].T.astype(
            jnp.bfloat16
        )

    @pl.when(step == pl.num_programs(0) - 1)
    def _():
        local_ref[...] = total[:per_dev]
        skip = total.shape[0] - far_ref.shape[0]

        @pl.loop(0, far_ref.shape[0])
        def _(i):
            held[i] = total[skip + i].astype(jnp.bfloat16)
            pltpu.make_async_copy(held.at[i], far_ref.at[i], sems.at[1]).start()

        pltpu.make_async_copy(held.at[pl.ds(0, far_ref.shape[0])], far_ref, sems.at[1]).wait()


def attend(table, valid, queries, grads, pool):
    pool_size = pool.shape[0]
    per_dev = QB_DEV
    far_size = pool_size - per_dev
    anywhere = pl.BlockSpec(memory_space=pl.ANY)
    tile = pl.BlockSpec((BLOCK, GROUP * HD), lambda i, *_: (i, 0))
    whole = lambda size: pl.BlockSpec((size, BLOCK, 2 * HD), lambda i, *_: (0, 0, 0), pipeline_mode=pl.Buffered(1))
    return pl.pallas_call(
        attend_kernel,
        grid_spec=pltpu.PrefetchScalarGridSpec(
            num_scalar_prefetch=2,
            grid=(per_dev,),
            in_specs=[tile, tile, anywhere],
            out_specs=[tile, whole(per_dev), anywhere],
            scratch_shapes=[
                pltpu.VMEM((pool_size, BLOCK, 2 * HD), jnp.float32),
                pltpu.VMEM((NKB * BLOCK, GROUP * BLOCK), jnp.float32),
                pltpu.VMEM((NKB * BLOCK, GROUP * BLOCK), jnp.float32),
                pltpu.VMEM((NKB * BLOCK, GROUP * BLOCK), jnp.bfloat16),
                pltpu.VMEM((NKB * BLOCK, HD), jnp.bfloat16),
                pltpu.VMEM((pool_size, BLOCK, 2 * HD), jnp.bfloat16),
                pltpu.SemaphoreType.DMA((2,)),
            ],
        ),
        out_shape=[
            jax.ShapeDtypeStruct(queries.shape, jnp.bfloat16),
            jax.ShapeDtypeStruct((per_dev, BLOCK, 2 * HD), jnp.float32),
            jax.ShapeDtypeStruct((far_size, BLOCK, 2 * HD), jnp.bfloat16),
        ],
        compiler_params=pltpu.CompilerParams(vmem_limit_bytes=62 << 20),
        name="attend",
    )(table, valid, queries, grads, pool)


def exchange(array):
    return lax.all_to_all(array, "ctx", split_axis=0, concat_axis=0, tiled=True)


def body(queries, keys, values, out_grad, rand_blocks, rand_count):
    heads = lax.axis_size("head")
    shards = lax.axis_size("ctx")
    myself = lax.axis_index("ctx")
    per_dev = QB_DEV
    entries = per_dev * RAND
    owners_used = min(entries, shards - 3)
    capacity = (entries + owners_used - 1) // owners_used
    total_blocks = per_dev * shards
    far_slots = shards * capacity
    piece = G * BLOCK // shards

    tokens = keys.shape[0]
    pairs = jnp.stack([keys.reshape(tokens, heads, HD), values.reshape(tokens, heads, HD)], axis=2)
    pairs = pairs.transpose(1, 0, 2, 3).reshape(heads, tokens, 2 * HD)
    local_rows = lax.all_to_all(pairs, "head", split_axis=0, concat_axis=0, tiled=True)
    local_rows = local_rows.reshape(heads * tokens, 2 * HD)
    local_pairs = local_rows.reshape(per_dev, BLOCK, 2 * HD)
    head_queries = lax.all_to_all(queries, "head", split_axis=1, concat_axis=0, tiled=True)
    head_grads = lax.all_to_all(out_grad, "head", split_axis=1, concat_axis=0, tiled=True)

    flat_blocks = rand_blocks.reshape(shards, entries)
    owners = flat_blocks // per_dev
    offsets = flat_blocks % per_dev
    positions = jnp.arange(entries, dtype=jnp.int32)
    earlier = positions[None, :] < positions[:, None]
    same_owner = owners[:, :, None] == owners[:, None, :]
    slot_ranks = jnp.sum(same_owner & earlier[None], axis=2)
    slot_range = jnp.arange(capacity, dtype=jnp.int32)
    send_hits = (
        (owners == myself)[:, None, :] & (slot_ranks[:, None, :] == slot_range[None, :, None])
    ).astype(jnp.float32)
    offset_hot = (
        offsets[:, :, None] == jnp.arange(per_dev, dtype=jnp.int32)[None, None, :]
    ).astype(jnp.float32)
    send_table = jnp.einsum("dme,deq->dmq", send_hits, offset_hot)
    targets = jnp.arange(shards, dtype=jnp.int32)[:, None, None]
    first_slot = (slot_range == 0)[None, :, None]
    block_range = jnp.arange(per_dev, dtype=jnp.int32)[None, None, :]
    right_send = (targets == (myself + 1) % shards) & first_slot & (block_range == per_dev - 1)
    left_send = (targets == (myself - 1 + shards) % shards) & first_slot & (block_range == 0)
    send_table = send_table + right_send.astype(jnp.float32) + left_send.astype(jnp.float32)
    left_far = per_dev + (myself - 1 + shards) % shards * capacity
    right_far = per_dev + (myself + 1) % shards * capacity
    outgoing = jnp.einsum(
        "dmq,qtc->dmtc",
        send_table.astype(jnp.bfloat16),
        local_pairs,
        preferred_element_type=jnp.float32,
    ).astype(jnp.bfloat16)
    pieces = local_rows[: G * BLOCK].reshape(shards, piece, 2 * HD)
    packed = jnp.concatenate([outgoing.reshape(shards, capacity * BLOCK, 2 * HD), pieces], axis=1)
    arrived = exchange(packed)
    far_pairs = arrived[:, : capacity * BLOCK].reshape(far_slots, BLOCK, 2 * HD)
    my_piece = jnp.broadcast_to(arrived[0, capacity * BLOCK :][None], (shards, piece, 2 * HD))
    global_pairs = exchange(my_piece).reshape(G, BLOCK, 2 * HD)
    pool = jnp.concatenate([local_pairs, far_pairs, global_pairs], axis=0)

    edge_base = per_dev + far_slots
    local_index = jnp.arange(per_dev, dtype=jnp.int32)
    seq_block = myself * per_dev + local_index
    left_index = jnp.where(local_index > 0, local_index - 1, left_far)
    right_index = jnp.where(local_index < per_dev - 1, local_index + 1, right_far)
    global_index = jnp.broadcast_to(
        edge_base + jnp.arange(G, dtype=jnp.int32)[None, :], (per_dev, G)
    )
    my_owners = lax.dynamic_index_in_dim(owners, myself, 0, keepdims=False)
    my_ranks = lax.dynamic_index_in_dim(slot_ranks, myself, 0, keepdims=False)
    random_index = (per_dev + my_owners * capacity + my_ranks).reshape(per_dev, RAND)
    key_table = jnp.concatenate(
        [jnp.stack([left_index, local_index, right_index], axis=1), global_index, random_index],
        axis=1,
    ).astype(jnp.int32)
    my_counts = lax.dynamic_slice_in_dim(rand_count, myself * per_dev, per_dev)
    key_valid = jnp.concatenate(
        [
            jnp.stack([seq_block > 0, seq_block >= 0, seq_block < total_blocks - 1], axis=1),
            jnp.ones((per_dev, G), bool),
            jnp.arange(RAND, dtype=jnp.int32)[None, :] < my_counts[:, None],
        ],
        axis=1,
    ).astype(jnp.int32)

    query_grad, local_grads, far_grads = attend(key_table, key_valid, head_queries, head_grads, pool)

    packed_grads = jnp.concatenate(
        [
            far_grads[:far_slots].reshape(shards, capacity * BLOCK, 2 * HD),
            far_grads[far_slots:].reshape(shards, piece, 2 * HD),
        ],
        axis=1,
    )
    returned = exchange(packed_grads)
    returned_far = returned[:, : capacity * BLOCK].reshape(shards, capacity, BLOCK, 2 * HD)
    global_piece = jnp.sum(returned[:, capacity * BLOCK :].astype(jnp.float32), axis=0)
    global_piece = jnp.broadcast_to(global_piece[None].astype(jnp.bfloat16), (shards, piece, 2 * HD))
    global_total = exchange(global_piece).reshape(G, BLOCK, 2 * HD).astype(jnp.float32)
    local_grads = local_grads + jnp.einsum(
        "dmq,dmtc->qtc",
        send_table.astype(jnp.bfloat16),
        returned_far,
        preferred_element_type=jnp.float32,
    )
    local_grads = local_grads.at[:G].add(
        jnp.where(myself == 0, global_total, jnp.zeros_like(global_total))
    )
    key_grad = local_grads[:, :, :HD].reshape(per_dev * BLOCK, HD).astype(jnp.bfloat16)
    value_grad = local_grads[:, :, HD:].reshape(per_dev * BLOCK, HD).astype(jnp.bfloat16)
    return (query_grad, key_grad, value_grad)


MESH = pl.DeviceIdType.MESH
LINE = 4
SHARD = QB_DEV * BLOCK
ENTRIES = QB_DEV * RAND
CAP = 2
COLUMN = 2 * LINE
DENSE = COLUMN * QB_DEV
SPARSE = COLUMN * CAP
POOL = DENSE + SPARSE + G
HALF = QB_DEV // 2
WINDOW = QB_DEV + 2
WIDE = GROUP * HD
TILE = 16
SPOT, SOURCE, WANTED, GIVEN = 0, 32, 96, 128


def place():
    me = lax.axis_index("ctx")
    return me // 4, (me // 2) % 2, me % 2


def index_of(z, y, c):
    return z * 4 + y * 2 + c


def remote(src, dst, send_sem, recv_sem, **device):
    return pltpu.make_async_remote_copy(
        src_ref=src, dst_ref=dst, send_sem=send_sem, recv_sem=recv_sem, device_id=device, device_id_type=MESH
    )


def greet(z, y, c, head):
    barrier = pltpu.get_barrier_semaphore()

    def tell(**device):
        pl.semaphore_signal(barrier, inc=1, device_id=device, device_id_type=MESH)

    tell(ctx=index_of(z, 1 - y, c))
    tell(ctx=index_of(z, 1 - y, 1 - c))
    tell(ctx=index_of(z, y, 1 - c))
    tell(head=1 - head)

    @pl.when(z > 0)
    def _():
        tell(ctx=index_of(z - 1, y, c))

    @pl.when(z < LINE - 1)
    def _():
        tell(ctx=index_of(z + 1, y, c))

    pl.semaphore_wait(barrier, 4 + (z + 2) // 3 + (5 - z) // 3)


def listed(table, user, owner, missing, by_entry=False):
    first = jnp.int32(missing)
    second = jnp.int32(missing)
    seen = jnp.int32(0)
    for e in range(ENTRIES):
        offset = table[e % RAND, user * QB_DEV + e // RAND] - owner * QB_DEV
        hit = ((offset >= 0) & (offset < QB_DEV)).astype(jnp.int32)
        value = e if by_entry else offset
        second = jnp.where(hit * seen > 0, value, second)
        first = jnp.where(hit * (1 - seen) > 0, value, first)
        seen = jnp.maximum(seen, hit)
    if not by_entry:
        first = jnp.where(user == owner + 1, QB_DEV - 1, first)
        first = jnp.where(user == owner - 1, 0, first)
    return first, second


def stacked(ref, b):
    rows = pl.ds(pl.multiple_of(b * BLOCK, BLOCK), BLOCK)
    return jnp.concatenate([ref[rows, h * HD : (h + 1) * HD] for h in range(GROUP)], axis=0)


def masked(tile, use):
    return tile + jnp.where(use, 0.0, -jnp.inf).astype(jnp.float32)


def column_max(tile):
    return jnp.max(tile, axis=0, keepdims=True)


def column_sum(tile):
    return jnp.sum(tile, axis=0, keepdims=True)


def window_rows(b):
    return pl.ds(pl.multiple_of(b * BLOCK, BLOCK), 3 * BLOCK)


TOP_W, SUM_W, TOP_E, SUM_E, SCALE_W, SCALE_E, PART, DOT = (slice(i, i + 1) for i in range(8))


def window_scores(b, block, blocks, queries, window, weights, stats):
    tile = dot(window[0, window_rows(b), :], stacked(queries, b), CONTRACT_LAST)
    tiles = [tile[i * BLOCK : (i + 1) * BLOCK] for i in range(3)]
    tiles[0] = masked(tiles[0], block > 0)
    tiles[2] = masked(tiles[2], block < blocks - 1)
    top = column_max(jnp.maximum(jnp.maximum(tiles[0], tiles[1]), tiles[2]))
    row_sum = jnp.zeros_like(top)
    for i in range(3):
        weight = jnp.exp2((tiles[i] - top) * EXP_FACTOR)
        row_sum += column_sum(weight)
        weights[b, i * BLOCK : (i + 1) * BLOCK, :] = weight
    stats[b, TOP_W, :] = top
    stats[b, SUM_W, :] = row_sum


def edge_scores(b, queries, edge, weights, stats):
    tile = dot(edge[0], stacked(queries, b), CONTRACT_LAST)
    top = column_max(tile)
    weight = jnp.exp2((tile - top) * EXP_FACTOR)
    weights[b] = weight
    stats[b, TOP_E, :] = top
    stats[b, SUM_E, :] = column_sum(weight)


def listed_scores(b, count, marks, queries, grads, keys, weights, stats, sent):
    query, grad = stacked(queries, b), stacked(grads, b)
    window_top, edge_top = stats[b, TOP_W, :], stats[b, TOP_E, :]
    top = jnp.maximum(window_top, edge_top)
    tiles = []
    for r in range(RAND):
        tile = masked(dot(keys[marks[SPOT + b * RAND + r]], query, CONTRACT_LAST), r < count)
        tiles.append(tile)
        top = jnp.maximum(top, column_max(tile))
    window_part = jnp.exp2((window_top - top) * EXP_FACTOR)
    edge_part = jnp.exp2((edge_top - top) * EXP_FACTOR)
    row_sum = window_part * stats[b, SUM_W, :] + edge_part * stats[b, SUM_E, :]
    for r in range(RAND):
        tiles[r] = jnp.exp2((tiles[r] - top) * EXP_FACTOR)
        row_sum += column_sum(tiles[r])
    scale = 1.0 / row_sum
    stats[b, SCALE_W, :] = window_part * scale
    stats[b, SCALE_E, :] = edge_part * scale
    for r in range(RAND):
        weight = tiles[r] * scale
        weights[b, r * BLOCK : (r + 1) * BLOCK, :] = weight
        sent[1, b * RAND + r] = dot(weight.astype(jnp.bfloat16), grad).astype(jnp.bfloat16)


def edge_values(b, grads, weights, stats, edge_total):
    weight = weights[b] * stats[b, SCALE_E, :]
    edge_total[1] += dot(weight.astype(jnp.bfloat16), stacked(grads, b))


def window_values(b, grads, weights, stats, total):
    weight = weights[b] * stats[b, SCALE_W, :]
    total[1, window_rows(b), :] += dot(weight.astype(jnp.bfloat16), stacked(grads, b))


def window_dots(b, grads, window, weights, dprobs, stats):
    dprob = dot(window[1, window_rows(b), :], stacked(grads, b), CONTRACT_LAST)
    dprobs[b] = dprob
    stats[b, PART, :] = column_sum(weights[b] * dprob) * stats[b, SCALE_W, :]


def edge_dots(b, grads, edge, weights, dprobs, stats):
    dprob = dot(edge[1], stacked(grads, b), CONTRACT_LAST)
    dprobs[b] = dprob
    stats[b, PART, :] += column_sum(weights[b] * dprob) * stats[b, SCALE_E, :]


def listed_dots(b, marks, queries, grads, values, weights, stats, dscores, sent):
    query, grad = stacked(queries, b), stacked(grads, b)
    row_dot = stats[b, PART, :]
    dprobs = []
    for r in range(RAND):
        dprob = dot(values[marks[SPOT + b * RAND + r]], grad, CONTRACT_LAST)
        row_dot += column_sum(weights[b, r * BLOCK : (r + 1) * BLOCK, :] * dprob)
        dprobs.append(dprob)
    stats[b, DOT, :] = row_dot
    for r in range(RAND):
        weight = weights[b, r * BLOCK : (r + 1) * BLOCK, :]
        dscore = (weight * (dprobs[r] - row_dot)).astype(jnp.bfloat16)
        dscores[b, (5 + r) * BLOCK : (6 + r) * BLOCK, :] = dscore
        sent[0, b * RAND + r] = (dot(dscore, query) * FACTOR).astype(jnp.bfloat16)


def edge_keys(b, queries, weights, dprobs, stats, dscores, edge_total):
    weight = weights[b] * stats[b, SCALE_E, :]
    dscore = (weight * (dprobs[b] - stats[b, DOT, :])).astype(jnp.bfloat16)
    dscores[b, 3 * BLOCK : 5 * BLOCK, :] = dscore
    edge_total[0] += dot(dscore, stacked(queries, b)) * FACTOR


def window_keys(b, queries, weights, dprobs, stats, dscores, total):
    weight = weights[b] * stats[b, SCALE_W, :]
    dscore = (weight * (dprobs[b] - stats[b, DOT, :])).astype(jnp.bfloat16)
    dscores[b, : 3 * BLOCK, :] = dscore
    total[0, window_rows(b), :] += dot(dscore, stacked(queries, b)) * FACTOR


def query_part(b, marks, window, edge, listed_keys, dscores, dquery):
    keys = [window[0, window_rows(b), :], edge[0]]
    keys += [listed_keys[marks[SPOT + b * RAND + r]] for r in range(RAND)]
    grad = dot(jnp.concatenate(keys, axis=0), dscores[b], CONTRACT_FIRST) * FACTOR
    rows = pl.ds(pl.multiple_of(b * BLOCK, BLOCK), BLOCK)
    for h in range(GROUP):
        dquery[rows, h * HD : (h + 1) * HD] = grad[:, h * BLOCK : (h + 1) * BLOCK].T.astype(jnp.bfloat16)


def line_kernel(
    table, count, q_in, k_in, v_in, g_in, query_grad, key_grad, value_grad,
    marks, queries, grads, key_pool, value_pool, staged, packed, window, edge, stats,
    window_weights, window_dprobs, edge_weights, edge_dprobs, listed_weights, dscores,
    sent, outbox, total, edge_total, edge_out, edge_in, edge_sum, beside_in, across_in, z_out, z_in, dquery, dpair,
    local_sem, stage_sem, head_send, head_recv, up_send, down_send, gz_recv, gy_send, gy_recv, gc_send, gc_recv,
    ge_send, ge_recv, rc_send, rc_recv, ry_send, ry_recv, re_send, re_recv, rz_send, rz_recv, out_sem,
):
    z, y, c = place()
    me = index_of(z, y, c)
    head = lax.axis_index("head")
    other = 1 - head
    tokens = q_in.shape[0]
    blocks = table.shape[1]
    first_block = me * QB_DEV
    pools = (key_pool, value_pool)

    def line_of(zz, cc):
        return (zz * 2 + cc) * QB_DEV

    token_rows = pl.ds(pl.multiple_of(head * tokens, tokens), tokens)
    arrivals = pl.ds(line_of(z, c) + head * HALF, HALF)

    def lane(side, width):
        return pl.ds(pl.multiple_of(side * width, width), width)

    def keep_pair(kv):
        src = (k_in, v_in)[kv].at[:, :, lane(head, HD)]
        return pltpu.make_async_copy(src, pools[kv].at[arrivals], local_sem.at[kv])

    def stage_pair(kv):
        src = (k_in, v_in)[kv].at[:, :, lane(other, HD)]
        return pltpu.make_async_copy(src, staged.at[kv], stage_sem.at[kv])

    def swap_pair(kv):
        return remote(staged.at[kv], pools[kv].at[arrivals], head_send.at[kv], head_recv.at[kv], head=other)

    def keep_wide(i):
        src, dst = ((q_in, queries), (g_in, grads))[i]
        return pltpu.make_async_copy(src.at[:, lane(head, WIDE)], dst.at[token_rows, :], local_sem.at[2 + i])

    def swap_wide(i):
        src, dst = ((q_in, queries), (g_in, grads))[i]
        return remote(
            src.at[:, lane(other, WIDE)], dst.at[token_rows, :], head_send.at[2 + i], head_recv.at[2 + i], head=other
        )

    for kv in range(2):
        keep_pair(kv).start()
        stage_pair(kv).start()
    for i in range(2):
        keep_wide(i).start()
    greet(z, y, c, head)
    for kv in range(2):
        stage_pair(kv).wait()
        swap_pair(kv).start()

    def quarter(zz, u, kv):
        return pools[kv].at[pl.ds(line_of(zz, c) + u * HALF, HALF)], (zz * 2 + u) * 2 + kv

    def up(zz, u, kv):
        part, i = quarter(zz, u, kv)
        return remote(part, part, up_send.at[i], gz_recv.at[i], ctx=index_of((z + 1) % LINE, y, c))

    def down(zz, u, kv):
        part, i = quarter(zz, u, kv)
        return remote(part, part, down_send.at[i], gz_recv.at[i], ctx=index_of((z + 3) % LINE, y, c))

    def beside(zz, kv):
        part = pools[kv].at[pl.ds(line_of(zz, c), QB_DEV)]
        i = zz * 2 + kv
        return remote(part, part, gc_send.at[i], gc_recv.at[i], ctx=index_of(z, y, 1 - c))

    def across(zz, kv, d, sender):
        slots = pools[kv].at[pl.ds(DENSE + (zz * 2 + sender) * CAP, CAP)]
        i = zz * 2 + kv
        return remote(packed.at[zz, kv, d], slots, gy_send.at[d, i], gy_recv.at[sender, i], ctx=index_of(z, 1 - y, d))

    edge_slots = pl.ds(DENSE + SPARSE, G)

    def edge_across(kv):
        return remote(
            pools[kv].at[pl.ds(0, G)], pools[kv].at[edge_slots], ge_send.at[kv], ge_recv.at[kv],
            ctx=index_of(z, 1 - y, 0),
        )

    def edge_beside(kv):
        part = pools[kv].at[edge_slots]
        return remote(part, part, ge_send.at[kv], ge_recv.at[kv], ctx=index_of(z, y, 1 - c))

    first_edge = (y == 0) & (c == 0)

    def complete(zz, kv):
        @pl.when((zz == 0) & first_edge)
        def _():
            edge_across(kv).start()

        wanted = [marks[WANTED + zz * 4 + s] for s in range(2 * CAP)]
        line = line_of(zz, c)

        @pl.loop(0, BLOCK // TILE, unroll=2)
        def _(i):
            rows = pl.ds(pl.multiple_of(i * TILE, TILE), TILE)
            tiles = [pools[kv][line + q, rows, :] for q in range(QB_DEV)]
            for s, want in enumerate(wanted):
                tile = tiles[0]
                for q in range(1, QB_DEV):
                    tile = jnp.where(want == q, tiles[q], tile)
                packed[zz, kv, s // CAP, s % CAP, rows, :] = tile

        for d in range(2):
            across(zz, kv, d, c).start()
        beside(zz, kv).start()

    def pass_on(zz, u, kv, upward, downward):
        if upward:

            @pl.when(z < LINE - 1)
            def _():
                up(zz, u, kv).start()

        if downward:

            @pl.when(z > 0)
            def _():
                down(zz, u, kv).start()

    def hop(j, u, kv):
        @pl.when(z - j >= 0)
        def _():
            up(z - j, u, kv).wait_recv()
            pass_on(z - j, u, kv, True, False)

        @pl.when(z + j <= LINE - 1)
        def _():
            down(z + j, u, kv).wait_recv()
            pass_on(z + j, u, kv, False, True)

    def done(j, kv):
        @pl.when(z - j >= 0)
        def _():
            complete(z - j, kv)

        @pl.when(z + j <= LINE - 1)
        def _():
            complete(z + j, kv)

    for kv in range(2):
        keep_pair(kv).wait()
        pass_on(z, head, kv, True, True)
    @pl.loop(0, LINE)
    def _(zz):
        for d in range(2):
            pair = listed(table, index_of(z, 1 - y, d), index_of(zz, y, c), 0)
            for k in range(CAP):
                marks[WANTED + zz * 4 + d * CAP + k] = pair[k]

    swap_pair(0).wait_recv()
    pass_on(z, other, 0, True, True)
    swap_wide(0).start()
    hop(1, head, 0)
    complete(z, 0)
    swap_pair(1).wait_recv()
    pass_on(z, other, 1, True, True)
    swap_wide(1).start()
    complete(z, 1)
    hop(1, other, 0)
    done(1, 0)
    hop(1, head, 1)
    hop(1, other, 1)
    done(1, 1)

    owners = []
    for e in range(ENTRIES):
        named = table[e % RAND, first_block + e // RAND]
        owner = named // QB_DEV
        rank = jnp.int32(0)
        for before in owners:
            rank += (before == owner).astype(jnp.int32)
        owners.append(owner)
        line = (owner // 4) * 2 + owner % 2
        same = (owner // 2) % 2 == y
        marks[SPOT + e] = jnp.where(same, line * QB_DEV + named - owner * QB_DEV, DENSE + line * CAP + rank)

    @pl.loop(0, 4 * LINE)
    def _(owner):
        pair = listed(table, me, owner, 0, by_entry=True)
        for k in range(CAP):
            marks[SOURCE + owner * CAP + k] = pair[k]

    @pl.loop(0, LINE)
    def _(zz):
        users = (me, index_of(z, y, 1 - c), index_of(z, 1 - y, 0), index_of(z, 1 - y, 1))
        for i, user in enumerate(users):
            pair = listed(table, user, index_of(zz, y, c), -1)
            for k in range(CAP):
                marks[GIVEN + zz * 8 + i * CAP + k] = pair[k]

    hop(2, head, 0)
    hop(2, other, 0)
    done(2, 0)
    hop(2, head, 1)
    hop(2, other, 1)
    done(2, 1)

    near = z + jnp.where(c == 0, y - 1, y)
    has_near = (near >= 0) & (near < LINE)
    near_slot = DENSE + (near * 2 + 1 - c) * CAP
    mine = line_of(z, c)
    left = jnp.where(c == 1, line_of(z, 0) + QB_DEV - 1, jnp.where(has_near, near_slot, mine))
    right = jnp.where(c == 0, line_of(z, 1), jnp.where(has_near, near_slot, mine))

    def fill_window(kv):
        beside(z, kv).wait_recv()

        @pl.when(has_near)
        def _():
            across(near, kv, 0, 1 - c).wait_recv()

        window[kv, :BLOCK, :] = pools[kv][left]
        for q in range(QB_DEV):
            window[kv, (q + 1) * BLOCK : (q + 2) * BLOCK, :] = pools[kv][mine + q]
        window[kv, (WINDOW - 1) * BLOCK :, :] = pools[kv][right]

    def fill_edge(kv):
        for zz in range(LINE):

            @pl.when(zz != z)
            def _():
                beside(zz, kv).wait_recv()

        @pl.when(y == 1)
        def _():
            edge_across(kv).wait_recv()

        @pl.when((y == 1) & (c == 0))
        def _():
            edge_beside(kv).start()

        spot = jnp.where(y == 0, 0, DENSE + SPARSE)
        for g in range(G):
            edge[kv, g * BLOCK : (g + 1) * BLOCK, :] = pools[kv][spot + g]

    def slots_arrived(kv):
        for zz in range(LINE):
            for sender in range(2):

                @pl.when((zz != near) | (sender == c))
                def _():
                    across(zz, kv, 0, sender).wait_recv()

    total[...] = jnp.zeros_like(total)
    edge_total[...] = jnp.zeros_like(edge_total)
    edge_sum[...] = jnp.zeros_like(edge_sum)
    hop(3, head, 0)
    hop(3, other, 0)
    done(3, 0)
    fill_window(0)
    keep_wide(0).wait()
    swap_wide(0).wait_recv()

    @pl.loop(0, QB_DEV)
    def _(b):
        window_scores(b, first_block + b, blocks, queries, window, window_weights, stats)

    fill_edge(0)

    @pl.loop(0, QB_DEV)
    def _(b):
        edge_scores(b, queries, edge, edge_weights, stats)

    hop(3, head, 1)
    hop(3, other, 1)
    done(3, 1)
    slots_arrived(0)
    keep_wide(1).wait()
    swap_wide(1).wait_recv()

    @pl.loop(0, QB_DEV, unroll=2)
    def _(b):
        listed_scores(
            b, count[first_block + b], marks, queries, grads, key_pool, listed_weights, stats, sent
        )

    def window_value_sums(b):
        window_values(b, grads, window_weights, stats, total)

    def window_key_sums(b):
        window_keys(b, queries, window_weights, window_dprobs, stats, dscores, total)

    def fill_outbox(kv):
        @pl.loop(0, 4 * LINE * CAP)
        def _(s):
            outbox[kv, s] = sent[kv, marks[SOURCE + s]]

    def fill_near(kv):
        @pl.when(me > 0)
        def _():
            outbox[kv, (me - 1) * CAP] = total[kv, :BLOCK, :].astype(jnp.bfloat16)

        @pl.when(me < 4 * LINE - 1)
        def _():
            outbox[kv, (me + 1) * CAP] = total[kv, (WINDOW - 1) * BLOCK :, :].astype(jnp.bfloat16)

    def out_slots(zz, yy, cc, kv):
        return outbox.at[kv, pl.ds(index_of(zz, yy, cc) * CAP, CAP)]

    def give_beside(zz, kv):
        i = zz * 2 + kv
        return remote(
            out_slots(zz, y, 1 - c, kv), beside_in.at[zz, kv], rc_send.at[i], rc_recv.at[i], ctx=index_of(z, y, 1 - c)
        )

    def give_across(zz, kv, d, sender):
        i = zz * 2 + kv
        return remote(
            out_slots(zz, 1 - y, d, kv), across_in.at[sender, zz, kv],
            ry_send.at[d, i], ry_recv.at[sender, i], ctx=index_of(z, 1 - y, d),
        )

    def give_edge_beside(kv):
        return remote(
            edge_out.at[kv], edge_in.at[0, kv], re_send.at[kv], re_recv.at[0, kv], ctx=index_of(z, y, 1 - c)
        )

    def give_edge_across(kv):
        return remote(
            edge_out.at[kv], edge_in.at[1, kv], re_send.at[kv], re_recv.at[1, kv], ctx=index_of(z, 1 - y, c)
        )

    def half_unit(zz, kv, half):
        return pl.ds(pl.multiple_of(half * (SHARD // 2), SHARD // 2), SHARD // 2), (zz * 2 + kv) * 2 + half

    def give_up(zz, kv, half):
        rows, i = half_unit(zz, kv, half)
        return remote(
            z_out.at[zz, kv, rows, :], z_in.at[0, zz, kv, rows, :], rz_send.at[i], rz_recv.at[0, i],
            ctx=index_of((z + 1) % LINE, y, c),
        )

    def give_down(zz, kv, half):
        rows, i = half_unit(zz, kv, half)
        return remote(
            z_out.at[zz, kv, rows, :], z_in.at[1, zz, kv, rows, :], rz_send.at[i], rz_recv.at[1, i],
            ctx=index_of((z + 3) % LINE, y, c),
        )

    def pick(options):
        return jnp.where(z == 0, options[0], jnp.where(z == 1, options[1], jnp.where(z == 2, options[2], options[3])))

    order = [pick(options) for options in ((3, 3, 0, 0), (2, 0, 3, 1), (1, 2, 1, 2))] + [z]

    def give(i, kv):
        for d in range(2):
            give_across(order[i], kv, d, c).start()
        give_beside(order[i], kv).start()

    def give_edges(kv):
        @pl.when(c == 1)
        def _():
            edge_out[kv] = edge_total[kv].astype(jnp.bfloat16)
            give_edge_beside(kv).start()

    def sum_edges(kv):
        @pl.when(c == 0)
        def _():
            give_edge_beside(kv).wait_recv()
            edge_sum[kv] = edge_total[kv] + edge_in[0, kv].astype(jnp.float32)

        @pl.when((c == 0) & (y == 1))
        def _():
            edge_out[kv] = edge_sum[kv].astype(jnp.bfloat16)
            give_edge_across(kv).start()

    def take(i, kv, before=None):
        zz = order[i]
        before = None if before is None else (order[before[0]], before[1])
        last = i == LINE - 1
        give_beside(zz, kv).wait_recv()
        for d in range(2):
            give_across(zz, kv, 0, d).wait_recv()
        wanted = [marks[GIVEN + zz * 8 + s] for s in range(4 * CAP)]
        slots = index_of(zz, y, c) * CAP
        at_edge = first_edge & (zz == 0)

        below = (zz >= z if last else zz > z) & (z > 0)
        above = (zz <= z if last else zz < z) & (z < LINE - 1)

        @pl.loop(0, 2)
        def _(turn):
            half = 1 - turn

            @pl.when(at_edge & (half == 0))
            def _():
                give_edge_across(kv).wait_recv()
                edge_sum[kv] += edge_in[1, kv].astype(jnp.float32)

            @pl.when(below)
            def _():
                give_up(zz, kv, half).wait_recv()

            @pl.when(above)
            def _():
                give_down(zz, kv, half).wait_recv()

            @pl.loop(0, BLOCK // TILE, unroll=2)
            def _(t):
                row = pl.multiple_of(t * TILE, TILE)
                tile_rows = pl.ds(row, TILE)
                tiles = [outbox[kv, slots + k, tile_rows, :] for k in range(CAP)]
                for ref in (beside_in.at[zz, kv], across_in.at[0, zz, kv], across_in.at[1, zz, kv]):
                    tiles += [ref[k, tile_rows, :] for k in range(CAP)]
                tiles = [tile.astype(jnp.float32) for tile in tiles]
                for i in range(HALF):
                    q = half * HALF + i
                    rows = pl.ds(pl.multiple_of(q * BLOCK + row, TILE), TILE)
                    sums = jnp.where(below, z_in[0, zz, kv, rows, :].astype(jnp.float32), 0.0)
                    sums += jnp.where(above, z_in[1, zz, kv, rows, :].astype(jnp.float32), 0.0)
                    if last:
                        sums += total[kv, pl.ds(pl.multiple_of((q + 1) * BLOCK + row, TILE), TILE), :]
                    for want, tile in zip(wanted, tiles):
                        sums += jnp.where(want == q, tile, 0.0)
                    if i < G:
                        edge_rows = pl.ds(pl.multiple_of(i * BLOCK + row, TILE), TILE)
                        sums += jnp.where(at_edge & (half == 0), edge_sum[kv, edge_rows, :], 0.0)
                    sums = sums.astype(jnp.bfloat16)
                    if last:
                        dpair[kv, rows, :] = sums
                    else:
                        z_out[zz, kv, rows, :] = sums

            if not last:
                if before is not None:
                    give_up(*before, half).wait_send()

                @pl.when(zz > z)
                def _():
                    give_up(zz, kv, half).start()

                @pl.when(zz < z)
                def _():
                    give_down(zz, kv, half).start()

    def query_sums(b):
        query_part(b, marks, window, edge, key_pool, dscores, dquery)
        keep_query(b).start()

    def keep_query(b):
        rows = pl.ds(pl.multiple_of(b * BLOCK, BLOCK), BLOCK)
        return pltpu.make_async_copy(dquery.at[rows, :], query_grad.at[rows, :], out_sem.at[b])

    def keep_result(kv):
        return pltpu.make_async_copy(dpair.at[kv], (key_grad, value_grad)[kv], out_sem.at[QB_DEV + kv])

    at_end = (z == 0) | (z == LINE - 1)

    fill_outbox(1)
    give(0, 1)

    @pl.loop(0, QB_DEV)
    def _(b):
        edge_values(b, grads, edge_weights, stats, edge_total)

    give_edges(1)

    @pl.loop(0, QB_DEV)
    def _(b):
        window_value_sums(b)

    fill_near(1)
    sum_edges(1)
    give(1, 1)
    fill_window(1)

    @pl.loop(0, QB_DEV)
    def _(b):
        window_dots(b, grads, window, window_weights, window_dprobs, stats)

    fill_edge(1)

    @pl.loop(0, QB_DEV)
    def _(b):
        edge_dots(b, grads, edge, edge_weights, edge_dprobs, stats)

    @pl.when(at_end)
    def _():
        take(0, 1)

    give(2, 1)
    slots_arrived(1)

    @pl.loop(0, QB_DEV, unroll=2)
    def _(b):
        listed_dots(b, marks, queries, grads, value_pool, listed_weights, stats, dscores, sent)

    fill_outbox(0)
    give(0, 0)

    def edge_key_sums():
        @pl.loop(0, QB_DEV)
        def _(b):
            edge_keys(b, queries, edge_weights, edge_dprobs, stats, dscores, edge_total)

        give_edges(0)

    @pl.when(jnp.logical_not(at_end))
    def _():
        edge_key_sums()
        take(0, 1)

    take(1, 1)

    @pl.when(at_end)
    def _():
        edge_key_sums()

    @pl.loop(0, QB_DEV)
    def _(b):
        window_key_sums(b)

    fill_near(0)
    sum_edges(0)
    give(1, 0)
    query_sums(0)
    take(2, 1, (0, 1))
    query_sums(1)
    query_sums(2)
    give(2, 0)
    take(0, 0, (1, 1))
    query_sums(3)
    give(3, 1)
    query_sums(4)
    take(1, 0, (2, 1))
    give(3, 0)
    query_sums(5)
    take(2, 0, (0, 0))
    take(3, 1)
    keep_result(1).start()
    take(3, 0)
    keep_result(0).start()

    for half in range(2):
        give_up(order[2], 0, half).wait_send()
        give_up(order[1], 0, half).wait_send()
    for zz in range(LINE):
        for kv in range(2):
            beside(zz, kv).wait_send()
            give_beside(zz, kv).wait_send()
            for d in range(2):
                across(zz, kv, d, c).wait_send()
                give_across(zz, kv, d, c).wait_send()

            for u in range(2):

                @pl.when((z < LINE - 1) & (zz <= z))
                def _():
                    up(zz, u, kv).wait_send()

                @pl.when((z > 0) & (zz >= z))
                def _():
                    down(zz, u, kv).wait_send()

    for kv in range(2):

        @pl.when(c == 1)
        def _():
            give_edge_beside(kv).wait_send()

        @pl.when((c == 0) & (y == 1))
        def _():
            give_edge_across(kv).wait_send()
            edge_beside(kv).wait_send()

        @pl.when(first_edge)
        def _():
            edge_across(kv).wait_send()

        swap_wide(kv).wait_send()
        swap_pair(kv).wait_send()
    for b in range(QB_DEV):
        keep_query(b).wait()
    for kv in range(2):
        keep_result(kv).wait()


def settle_kernel(*refs):
    sources, targets, held, in_sem, out_sem = refs[:3], refs[3:6], refs[6:9], refs[9], refs[10]
    copies = []
    for src, dst, mid in zip(sources, targets, held):
        step = 2 * BLOCK
        for i in range(src.shape[0] // step):
            rows, n = pl.ds(i * step, step), len(copies)
            copies.append(
                (
                    pltpu.make_async_copy(src.at[rows, :], mid.at[rows, :], in_sem.at[n]),
                    pltpu.make_async_copy(mid.at[rows, :], dst.at[rows, :], out_sem.at[n]),
                )
            )
    for arrive, _ in copies:
        arrive.start()
    for arrive, leave in copies:
        arrive.wait()
        leave.start()
    for _, leave in copies:
        leave.wait()


def settle(arrays):
    anywhere = pl.BlockSpec(memory_space=pl.ANY)
    dma = pltpu.SemaphoreType.DMA
    return pl.pallas_call(
        settle_kernel,
        in_specs=[anywhere] * 3,
        out_specs=[anywhere] * 3,
        out_shape=[jax.ShapeDtypeStruct(array.shape, array.dtype) for array in arrays],
        scratch_shapes=[pltpu.VMEM(array.shape, array.dtype) for array in arrays] + [dma((9,)), dma((9,))],
        compiler_params=pltpu.CompilerParams(vmem_limit_bytes=62 << 20),
        name="settle",
    )(*arrays)


def body_line(queries, keys, values, out_grad, rand_blocks, rand_count):
    anywhere = pl.BlockSpec(memory_space=pl.ANY)
    scalars = pl.BlockSpec(memory_space=pltpu.SMEM)
    dma = pltpu.SemaphoreType.DMA
    bf16, f32 = jnp.bfloat16, jnp.float32
    keys = keys.reshape(HALF, BLOCK, 2 * HD)
    values = values.reshape(HALF, BLOCK, 2 * HD)
    result = jax.ShapeDtypeStruct((SHARD, HD), bf16)
    pair = 2 * LINE
    grads = pl.pallas_call(
        line_kernel,
        in_specs=[scalars, scalars] + [anywhere] * 4,
        out_specs=[anywhere] * 3,
        out_shape=[jax.ShapeDtypeStruct((SHARD, WIDE), bf16), result, result],
        scratch_shapes=[
            pltpu.SMEM((192,), jnp.int32),
            pltpu.VMEM((SHARD, WIDE), bf16),
            pltpu.VMEM((SHARD, WIDE), bf16),
            pltpu.VMEM((POOL, BLOCK, HD), bf16),
            pltpu.VMEM((POOL, BLOCK, HD), bf16),
            pltpu.VMEM((2, HALF, BLOCK, HD), bf16),
            pltpu.VMEM((LINE, 2, 2, CAP, BLOCK, HD), bf16),
            pltpu.VMEM((2, WINDOW * BLOCK, HD), bf16),
            pltpu.VMEM((2, G * BLOCK, HD), bf16),
            pltpu.VMEM((QB_DEV, 8, WIDE), f32),
            pltpu.VMEM((QB_DEV, 3 * BLOCK, WIDE), f32),
            pltpu.VMEM((QB_DEV, 3 * BLOCK, WIDE), f32),
            pltpu.VMEM((QB_DEV, G * BLOCK, WIDE), f32),
            pltpu.VMEM((QB_DEV, G * BLOCK, WIDE), f32),
            pltpu.VMEM((QB_DEV, RAND * BLOCK, WIDE), f32),
            pltpu.VMEM((QB_DEV, NKB * BLOCK, WIDE), bf16),
            pltpu.VMEM((2, ENTRIES, BLOCK, HD), bf16),
            pltpu.VMEM((2, 4 * LINE * CAP, BLOCK, HD), bf16),
            pltpu.VMEM((2, WINDOW * BLOCK, HD), f32),
            pltpu.VMEM((2, G * BLOCK, HD), f32),
            pltpu.VMEM((2, G * BLOCK, HD), bf16),
            pltpu.VMEM((2, 2, G * BLOCK, HD), bf16),
            pltpu.VMEM((2, G * BLOCK, HD), f32),
            pltpu.VMEM((LINE, 2, CAP, BLOCK, HD), bf16),
            pltpu.VMEM((2, LINE, 2, CAP, BLOCK, HD), bf16),
            pltpu.VMEM((LINE, 2, SHARD, HD), bf16),
            pltpu.VMEM((2, LINE, 2, SHARD, HD), bf16),
            pltpu.VMEM((SHARD, WIDE), bf16),
            pltpu.VMEM((2, SHARD, HD), bf16),
            dma((4,)), dma((2,)), dma((4,)), dma((4,)), dma((2 * pair,)), dma((2 * pair,)), dma((2 * pair,)),
            dma((2, pair)), dma((2, pair)), dma((pair,)), dma((pair,)), dma((2,)), dma((2,)),
            dma((pair,)), dma((pair,)), dma((2, pair)), dma((2, pair)), dma((2,)), dma((2, 2)),
            dma((2 * pair,)), dma((2, 2 * pair)), dma((QB_DEV + 2,)),
        ],
        compiler_params=pltpu.CompilerParams(
            collective_id=0, has_side_effects=True, vmem_limit_bytes=62 << 20
        ),
        name="line",
    )(rand_blocks.T, rand_count, queries, keys, values, out_grad)
    return tuple(settle(grads))


def solution(mesh):
    line = mesh.shape["ctx"] == 4 * LINE and mesh.shape["head"] == 2
    placed = P(("ctx", "head"), None)
    return jax.shard_map(
        body_line if line else body,
        mesh=mesh,
        in_specs=(placed, placed, placed, placed, P(), P()),
        out_specs=(P("ctx", "head"), P("ctx", "head"), P("ctx", "head")),
        check_vma=False,
    )
```
